256 devices in a mesh: pts: 32 (over x_hi, z, core), dir: 8 (over x_lo, y).
Axes of the slice: x: 4 (x_hi: 2, x_lo: 2; x = x_hi * 2 + x_lo), y: 4, z: 8, core: 2. Of those that a mesh axis runs over, the one named last changes fastest.
Arguments:
- action: float32 [50, 32, 512, 256], P(None, 'dir', 'pts'), may hold values from 0 to 60, as said below
- currents: float32 [2, 512, 256], P(None, 'pts'), may hold values from -0.1 to 0.1, as said below
- land_mask: int32 [512, 256], P('pts'), may hold values 0 or 1
- group_speed: float32 [50], replicated, may hold values from 0.02 to 0.55
- group_ratio: float32 [50], replicated, may hold values from 0.5 to 1
- bin_weight: float32 [50], replicated, may hold values from 0.002 to 0.02
Outputs:
- new_action: float32 [50, 32, 512, 256], P(None, 'dir', 'pts')
- wave_force: float32 [2, 512, 256], P(None, 'pts')
The draws below stay inside these ranges and needn't reach their ends.
Inputs may be any that keep to these rules, and one draw needn't show every extreme that they name: Positive action densities. currents vary slowly from point to point.
All inputs are finite; a program needn't handle non-finite values. No bound on the sum of `land_mask` on one device may be relied on, other than what follows from the above.
Results may differ from the reference program's by a relative error of at most 0.00022.
Values sent between devices are 32-bit elements; how exact they have to be, the bound alone decides.
No kernel may reach another device: no remote copies, remote signals or barrier semaphores. Data moves between devices by JAX's collectives and lax.ppermute only.
A program may use at most 64 MiB of HBM per device.

```python
import math
import jax
import jax.numpy as jnp
from jax import lax

NF = 50
NDIR = 32
NY = 256
NX = 512


def draw_action(key, part):
    k_dir, k_rough, k_freq = jax.random.split(key, 3)
    center = jax.random.uniform(k_dir, (), jnp.float32, 1.2 * math.pi, 1.6 * math.pi)
    angles = jnp.arange(NDIR).astype(jnp.float32) * (2.0 * math.pi / NDIR)
    spread = jnp.exp(0.5 * jnp.cos(angles - center))
    roughness = jnp.exp(jax.random.uniform(k_rough, (NF, NDIR, NX, NY), jnp.float32, math.log(0.5), math.log(2.0)))
    levels = jnp.exp(jax.random.uniform(k_freq, (NF,), jnp.float32, -0.5, 0.5))
    return spread[None, :, None, None] * roughness * levels[:, None, None, None]


def draw_currents(key, part):
    k_wave, k_sign, k_phase, k_amp, k_rough = jax.random.split(key, 5)
    rows = jnp.arange(NX).astype(jnp.float32)[None, :, None]
    cols = jnp.arange(NY).astype(jnp.float32)[None, None, :]
    modes = 3
    wavelengths = jax.random.uniform(k_wave, (2, modes, 2), jnp.float32, 40.0, 80.0)
    signs = jnp.where(jax.random.uniform(k_sign, (2, modes, 2), jnp.float32) < 0.5, -1.0, 1.0)
    numbers = 2.0 * math.pi / wavelengths * signs
    phases = jax.random.uniform(k_phase, (2, modes), jnp.float32, 0.0, 2.0 * math.pi)
    amps = jax.random.uniform(k_amp, (2, modes), jnp.float32, 0.035, 0.05)
    rough_size = 0.002
    field = jnp.zeros((2, NX, NY), jnp.float32)
    for mode in range(modes):
        arg = numbers[:, mode, 0][:, None, None] * rows + numbers[:, mode, 1][:, None, None] * cols + phases[:, mode][:, None, None]
        field = field + amps[:, mode][:, None, None] * jnp.sin(arg)
    saturated = 0.095 * jnp.tanh(field / 0.05)
    rough = jax.random.uniform(k_rough, (2, NX, NY), jnp.float32, -rough_size, rough_size)
    return saturated + rough


def with_ends(values, own_key, smallest, high):
    place = [jax.random.randint(jax.random.fold_in(own_key, axis), (), 0, length) for axis, length in enumerate(values.shape)]
    longest = values.shape.index(max(values.shape))
    beside = place[:longest] + [(place[longest] + 1) % values.shape[longest]] + place[longest + 1:]
    return values.at[tuple(place)].set(smallest).at[tuple(beside)].set(high)


def setup_inputs(seed: int = 0) -> dict:
    key_of = jax.random.split(jax.random.key(seed), 7)
    action = draw_action(jax.random.fold_in(key_of[6], 71), 0)
    currents = draw_currents(jax.random.fold_in(key_of[6], 71), 0)
    land_mask = with_ends((jax.random.randint(key_of[2], (NX, NY), 0, 10) < 9).astype(jnp.int32), jax.random.fold_in(key_of[2], 1), 0, 1)
    group_speed = jnp.clip(jnp.exp(jax.random.uniform(key_of[3], (NF,), jnp.float32, math.log(0.02), math.log(0.55))), 0.02, 0.55)
    group_ratio = jnp.clip(jax.random.uniform(key_of[4], (NF,), jnp.float32, 0.5, 1.0), 0.5, 1.0)
    bin_weight = jnp.clip(jnp.exp(jax.random.uniform(key_of[5], (NF,), jnp.float32, math.log(0.002), math.log(0.02))), 0.002, 0.02)
    return dict(action=action, currents=currents, land_mask=land_mask, group_speed=group_speed, group_ratio=group_ratio, bin_weight=bin_weight)


def upwind(velocity, behind, in_front):
    return jnp.maximum(velocity, 0.0) * behind + jnp.minimum(velocity, 0.0) * in_front


def advance(extended, cur_u, cur_v, land_cells, cosine_terms, sine_terms, group_speed):
    speed_x = group_speed[:, None, None, None] * cosine_terms[None, :, None, None]
    speed_y = group_speed[:, None, None, None] * sine_terms[None, :, None, None]
    drift_x = speed_x + (0.5 * (cur_u[:-1] + cur_u[1:]))[None, None]
    flux_x = upwind(drift_x, extended[:, :, :-1], extended[:, :, 1:])
    middle = extended[:, :, 1:-1]
    side_v = jnp.pad(cur_v[1:-1], ((0, 0), (1, 1)))
    drift_y = speed_y + (0.5 * (side_v[:, :-1] + side_v[:, 1:]))[None, None]
    padded = jnp.pad(middle, ((0, 0), (0, 0), (0, 0), (1, 1)))
    flux_y = upwind(drift_y, padded[..., :-1], padded[..., 1:])
    change = (flux_x[:, :, 1:] - flux_x[:, :, :-1]) + (flux_y[..., 1:] - flux_y[..., :-1])
    return land_cells * (middle - change)


def row_slope(values):
    return 0.5 * (values[2:] - values[:-2])


def col_slope(values):
    padded = jnp.pad(values[1:-1], ((0, 0), (1, 1)))
    return 0.5 * (padded[:, 2:] - padded[:, :-2])


def shear_terms(ext_u, ext_v):
    return row_slope(ext_u), col_slope(ext_u), row_slope(ext_v), col_slope(ext_v)


def turn_rate(face_angles, shears, total_dirs):
    u_dx, u_dy, v_dx, v_dy = shears
    sines = jnp.sin(face_angles)[:, None, None]
    cosines = jnp.cos(face_angles)[:, None, None]
    scale = total_dirs / (2.0 * math.pi)
    return scale * (sines * cosines * (u_dx - v_dy) + sines * sines * u_dy - cosines * cosines * v_dx)


def refract(cycle_ext, turning):
    flux = upwind(turning[None], cycle_ext[:, :-1], cycle_ext[:, 1:])
    return cycle_ext[:, 1:-1] - (flux[:, 1:] - flux[:, :-1])


def stress_table(angles, bin_weight, group_ratio):
    cos_sq = (jnp.cos(angles) * jnp.cos(angles))[None]
    sin_sq = (jnp.sin(angles) * jnp.sin(angles))[None]
    cross = (jnp.sin(angles) * jnp.cos(angles))[None]
    ratio = group_ratio[:, None]
    weight = bin_weight[:, None]
    return jnp.stack([weight * (ratio * (1.0 + cos_sq) - 0.5), weight * ratio * cross, weight * (ratio * (1.0 + sin_sq) - 0.5)])


def wave_force_of(extended):
    first = -(row_slope(extended[0]) + col_slope(extended[1]))
    second = -(row_slope(extended[1]) + col_slope(extended[2]))
    return jnp.stack([first, second])


def reference(action, currents, land_mask, group_speed, group_ratio, bin_weight):
    land_cells = land_mask.astype(jnp.float32)
    step_angle = 2.0 * math.pi / NDIR
    angles = jnp.arange(NDIR).astype(jnp.float32) * step_angle
    ext_u = jnp.pad(currents[0], ((1, 1), (0, 0)))
    ext_v = jnp.pad(currents[1], ((1, 1), (0, 0)))
    shears = shear_terms(ext_u, ext_v)
    face_angles = (jnp.arange(NDIR + 1).astype(jnp.float32) - 0.5) * step_angle
    turning = turn_rate(face_angles, shears, NDIR)
    cosine_terms = jnp.cos(angles)
    sine_terms = jnp.sin(angles)

    def one_frequency(inputs):
        slab, speed = inputs
        spectra = land_cells * slab[None]
        for substep in range(2):
            extended = jnp.pad(spectra, ((0, 0), (0, 0), (1, 1), (0, 0)))
            spectra = advance(extended, ext_u, ext_v, land_cells, cosine_terms, sine_terms, speed[None])
        cycle_ext = jnp.concatenate([spectra[:, -1:], spectra, spectra[:, :1]], axis=1)
        return refract(cycle_ext, turning)[0]

    new_action = lax.map(one_frequency, (action, group_speed))
    stress = jnp.einsum("kfd,fdry->kry", stress_table(angles, bin_weight, group_ratio), new_action, precision=lax.Precision.HIGHEST)
    extended = jnp.pad(stress, ((0, 0), (1, 1), (0, 0)))
    return new_action, wave_force_of(extended)
```

```python
import math
import functools

import numpy as np
import jax
import jax.numpy as jnp
from jax import lax
from jax.sharding import PartitionSpec as P
from jax.experimental import pallas as pl
from jax.experimental.pallas import tpu as pltpu

F32 = jnp.float32
LANES = 128
SUB = 8


def iota_masks():
    s = lax.broadcasted_iota(jnp.int32, (SUB, LANES), 0)
    l = lax.broadcasted_iota(jnp.int32, (SUB, LANES), 1)
    return s, l


def roll(x, shift, axis):
    return pltpu.roll(x, shift, axis)


class Grid:
    def __init__(self):
        s, l = iota_masks()
        self.s = s
        self.first_row = s == 0
        self.last_row = s == SUB - 1
        self.first_col = l == 0
        self.last_col = l == LANES - 1

    def below(self, t, hi):
        n, m = len(t), len(t[0])
        moved = [[roll(t[r][c], SUB - 1, 0) for c in range(m)] for r in range(n)]
        return [
            [
                jnp.where(self.last_row, moved[r + 1][c] if r + 1 < n else hi[c], moved[r][c])
                for c in range(m)
            ]
            for r in range(n)
        ]

    def above(self, t, lo):
        n, m = len(t), len(t[0])
        moved = [[roll(t[r][c], 1, 0) for c in range(m)] for r in range(n)]
        return [
            [
                jnp.where(self.first_row, moved[r - 1][c] if r > 0 else lo[c], moved[r][c])
                for c in range(m)
            ]
            for r in range(n)
        ]

    def right(self, row):
        m = len(row)
        moved = [roll(v, LANES - 1, 1) for v in row]
        return [
            jnp.where(self.last_col, moved[c + 1] if c + 1 < m else 0.0, moved[c]) for c in range(m)
        ]

    def left(self, row, start):
        m = len(row)
        moved = [roll(v, 1, 1) for v in row]
        return [
            jnp.where(self.first_col, moved[c - 1] if c > 0 else start, moved[c]) for c in range(m)
        ]


def face_flux(c, behind, in_front):
    return c * jnp.where(c > 0.0, behind, in_front)


def col_change(g, row, gs, vb, vl):
    right = g.right(row)
    flux = [face_flux(gs + vb[c], row[c], right[c]) for c in range(len(row))]
    edge = jnp.minimum(gs + vl, 0.0) * row[0]
    left = g.left(flux, edge)
    return [flux[c] - left[c] for c in range(len(row))]


def advance(g, t, gc, gs, ub, ub0, vb, vl, land, lo, hi):
    n, m = len(t), len(t[0])
    ahead = g.below(t, hi)
    flux = [[face_flux(gc + ub[r][c], t[r][c], ahead[r][c]) for c in range(m)] for r in range(n)]
    start = [face_flux(gc + ub0[c], lo[c], t[0][c]) for c in range(m)]
    before = g.above(flux, start)
    out = []
    for r in range(n):
        dy = col_change(g, t[r], gs, vb[r], vl[r])
        out.append(
            [land[r][c] * (t[r][c] - ((flux[r][c] - before[r][c]) + dy[c])) for c in range(m)]
        )
    return out


def tiles(ref, *lead):
    rows, cols = ref.shape[-2] // SUB, ref.shape[-1] // LANES
    return [
        [ref[(*lead, pl.ds(r * SUB, SUB), pl.ds(c * LANES, LANES))] for c in range(cols)]
        for r in range(rows)
    ]


def put_tiles(ref, t, *lead):
    for r, row in enumerate(t):
        for c, v in enumerate(row):
            ref[(*lead, pl.ds(r * SUB, SUB), pl.ds(c * LANES, LANES))] = v


def spread_row(ref, cols, *index):
    *lead, row = index
    return [
        jnp.broadcast_to(ref[(*lead, pl.ds(row, 1), pl.ds(c * LANES, LANES))], (SUB, LANES))
        for c in range(cols)
    ]


def turning(shears, sine, cosine, total_dirs):
    ux, uy, vx, vy = shears
    scale = total_dirs / (2.0 * math.pi)
    return [
        [
            scale
            * (
                sine * cosine * (ux[r][c] - vy[r][c])
                + sine * sine * uy[r][c]
                - cosine * cosine * vx[r][c]
            )
            for c in range(len(ux[0]))
        ]
        for r in range(len(ux))
    ]


def half_sum(a, b):
    return [[0.5 * (x + y) for x, y in zip(p, q)] for p, q in zip(a, b)]


def half_diff(a, b):
    return [[0.5 * (x - y) for x, y in zip(p, q)] for p, q in zip(a, b)]


def shears_of(g, u, v, u_lo, u_hi, v_lo, v_hi):
    ux = half_diff(g.below(u, u_hi), g.above(u, u_lo))
    vx = half_diff(g.below(v, v_hi), g.above(v, v_lo))
    uy = half_diff([g.right(r) for r in u], [g.left(r, 0.0) for r in u])
    vy = half_diff([g.right(r) for r in v], [g.left(r, 0.0) for r in v])
    return ux, uy, vx, vy


COS, SIN, FCOS, FSIN = 0, 6, 12, 17
TABLE = 22


def angle_table(sectors, per):
    total = sectors * per
    step = 2.0 * math.pi / total
    out = np.zeros((sectors, TABLE), np.float64)
    for k in range(sectors):
        d = np.arange(-1, per + 1) + k * per
        out[k, COS : COS + per + 2] = np.cos(d * step)
        out[k, SIN : SIN + per + 2] = np.sin(d * step)
        face = (np.arange(per + 1) + k * per - 0.5) * step
        out[k, FCOS : FCOS + per + 1] = np.cos(face)
        out[k, FSIN : FSIN + per + 1] = np.sin(face)
    return out.astype(np.float32)


def rows_kernel(x_ref, cur_ref, land_ref, up_ref, dn_ref):
    i = pl.program_id(0)
    count = x_ref.shape[0] // 32
    last = up_ref.shape[1] - SUB
    for ref, rows in ((up_ref, (14, 15)), (dn_ref, (0, 1))):
        for k, row in enumerate(rows):
            land = [
                jnp.broadcast_to(
                    land_ref[pl.ds(row, 1), pl.ds(c * LANES, LANES)].astype(F32), (SUB, LANES)
                )
                for c in range(2)
            ]
            for q in range(count // SUB):
                for c in range(2):
                    start = q * SUB * 32 + (row // SUB * 2 + c) * SUB + row % SUB
                    v = x_ref[pl.ds(start, SUB, stride=32), :]
                    at = pl.multiple_of(i * count + q * SUB, SUB)
                    ref[k, pl.ds(at, SUB), pl.ds(c * LANES, LANES)] = v * land[c]

    @pl.when(i == 0)
    def _():
        for ref, rows in ((up_ref, (14, 15)), (dn_ref, (0, 1))):
            for k, row in enumerate(rows):
                ref[k, pl.ds(last, SUB), :] = jnp.zeros((SUB, 2 * LANES), F32)
                ref[k, pl.ds(last, 1), :] = cur_ref[0, pl.ds(row, 1), :]
                ref[k, pl.ds(last + 1, 1), :] = cur_ref[1, pl.ds(row, 1), :]
                ref[k, pl.ds(last + 2, 1), :] = land_ref[pl.ds(row, 1), :].astype(F32)


def pack_inner(g, a, b):
    low2 = g.s < 6
    first = jnp.where(low2, roll(a[0], 6, 0), roll(a[1], 6, 0))
    mid = jnp.where(g.s < 4, roll(a[1], 6, 0), roll(b[0], 2, 0))
    last = jnp.where(g.s < 2, roll(b[0], 2, 0), roll(b[1], 2, 0))
    return first, mid, last


def pack_outer(g, a, b):
    one = jnp.where(g.s < 2, a[0], roll(a[1], 4, 0))
    two = jnp.where(g.s < 6, roll(b[0], 4, 0), b[1])
    return jnp.where(g.s < 4, one, two)


def unpack(g, inner, outer):
    a, b, c = inner
    a2, b2, b6, c6, o4 = roll(a, 2, 0), roll(b, 2, 0), roll(b, 6, 0), roll(c, 6, 0), roll(outer, 4, 0)
    low2, low6 = g.s < 2, g.s < 6
    one = [jnp.where(low2, outer, a2), jnp.where(low2, a2, jnp.where(low6, b2, o4))]
    two = [jnp.where(low2, o4, jnp.where(low6, b6, c6)), jnp.where(low6, c6, outer)]
    return one, two


def ends_kernel(total, sec_ref, tab_ref, cg_ref, x0_ref, x3_ref, cur_ref, land_ref,
                prev_ref, next_ref, ub_s, vb_s, k_s):
    g = Grid()
    i = pl.program_id(0)
    sec = sec_ref[0]
    freqs = x0_ref.shape[0]
    zero = [jnp.zeros((SUB, LANES), F32)] * 2

    @pl.when(i == 0)
    def _():
        u, v = tiles(cur_ref, 0), tiles(cur_ref, 1)
        put_tiles(ub_s, half_sum(u, g.below(u, zero)))
        put_tiles(vb_s, half_sum(v, [g.right(r) for r in v]))
        sh = shears_of(g, u, v, zero, zero, zero, zero)
        for n, f in ((0, 0), (1, 4)):
            put_tiles(k_s, turning(sh, tab_ref[sec, FSIN + f], tab_ref[sec, FCOS + f], total), n)

    def one(pair, _):
        for n, (x_ref, out_ref, d) in enumerate(((x0_ref, prev_ref, 0), (x3_ref, next_ref, 3))):
            ends = []
            for h in range(2):
                f = pair * 2 + h
                cg = cg_ref[i * freqs + f]
                gc, gs = cg * tab_ref[sec, COS + 1 + d], cg * tab_ref[sec, SIN + 1 + d]
                ub, vb = tiles(ub_s), tiles(vb_s)
                vl = [0.5 * cur_ref[1, pl.ds(r * SUB, SUB), pl.ds(0, LANES)] for r in range(2)]
                land = [[m.astype(F32) for m in row] for row in tiles(land_ref)]
                t = tiles(x_ref, f, 0)
                t = [[land[r][c] * t[r][c] for c in range(2)] for r in range(2)]
                for _s in range(2):
                    t = advance(g, t, gc, gs, ub, zero, vb, vl, land, zero, zero)
                k = tiles(k_s, n)
                limit = jnp.minimum if d == 0 else jnp.maximum
                ends.append([[limit(k[r][c], 0.0) * t[r][c] for c in range(2)] for r in range(2)])
            for c in range(2):
                got = pack_inner(g, [ends[0][r][c] for r in range(2)], [ends[1][r][c] for r in range(2)])
                for q in range(3):
                    out_ref[pair, pl.ds(q * SUB, SUB), pl.ds(c * LANES, LANES)] = got[q]
        return 0

    lax.fori_loop(0, freqs // 2, one, 0)


def main_kernel(total, sec_ref, tab_ref, cg_ref, ratio_ref, weight_ref,
                x_ref, cgc_ref, cgs_ref, cur_ref, land_ref,
                top_ref, bot_ref, ownup_ref, owndn_ref, topf_ref, botf_ref,
                new_ref, prev_ref, next_ref, force_ref, brow_ref,
                ub_s, ub0_s, vb_s, k_s, fld_s, at_s, ab_s, r_s, b_s):
    g = Grid()
    i = pl.program_id(0)
    blocks = pl.num_programs(0)
    sec = sec_ref[0]
    freqs = x_ref.shape[0]
    dirs = x_ref.shape[1]

    @pl.when(i == 0)
    def _():
        u, v = tiles(cur_ref, 0), tiles(cur_ref, 1)
        um2, vm2, lm2 = (spread_row(topf_ref, 2, 0, n) for n in range(3))
        um1, vm1, lm1 = (spread_row(topf_ref, 2, 1, n) for n in range(3))
        up0, vp0, lp0 = (spread_row(botf_ref, 2, 0, n) for n in range(3))
        up1, vp1, lp1 = (spread_row(botf_ref, 2, 1, n) for n in range(3))
        u0 = spread_row(cur_ref, 2, 0, 0)
        u15 = spread_row(cur_ref, 2, 0, 15)
        put_tiles(ub_s, half_sum(u, g.below(u, up0)))
        put_tiles(vb_s, half_sum(v, [g.right(r) for r in v]))
        put_tiles(ub0_s, half_sum([um1], [u0]))
        put_tiles(fld_s, half_sum([um2], [um1]), 0)
        put_tiles(fld_s, half_sum([u15], [up0]), 1)
        put_tiles(fld_s, half_sum([up0], [up1]), 2)
        put_tiles(fld_s, half_sum([vm1], [g.right(vm1)]), 3)
        put_tiles(fld_s, half_sum([vp0], [g.right(vp0)]), 4)
        put_tiles(fld_s, [[0.5 * w for w in vm1]], 5)
        put_tiles(fld_s, [[0.5 * w for w in vp0]], 6)
        put_tiles(fld_s, [lm1], 7)
        put_tiles(fld_s, [lp0], 8)
        sh = shears_of(g, u, v, um1, up0, vm1, vp0)
        for f in range(dirs + 1):
            put_tiles(k_s, turning(sh, tab_ref[sec, FSIN + f], tab_ref[sec, FCOS + f], total), f)
        r_s[...] = jnp.zeros_like(r_s)
        b_s[...] = jnp.zeros_like(b_s)

    def field(n):
        return [fld_s[n, :, pl.ds(c * LANES, LANES)] for c in range(2)]

    for q in range(freqs * dirs // SUB):
        at = pl.ds(q * SUB, SUB)
        gc, gs = cgc_ref[at, :], cgs_ref[at, :]
        row = lambda ref, n: [ref[n, at, pl.ds(c * LANES, LANES)] for c in range(2)]
        for outer, mid, inner, ca, cb, nv, nl, nm, sign, out in (
            (row(top_ref, 0), row(top_ref, 1), row(owndn_ref, 0), field(0),
             [ub0_s[:, pl.ds(c * LANES, LANES)] for c in range(2)], 3, 5, 7, 1, at_s),
            (row(ownup_ref, 1), row(bot_ref, 0), row(bot_ref, 1), field(1), field(2), 4, 6, 8, 1, ab_s),
        ):
            fa = [face_flux(gc + ca[c], outer[c], mid[c]) for c in range(2)]
            fb = [face_flux(gc + cb[c], mid[c], inner[c]) for c in range(2)]
            dy = col_change(g, mid, gs, field(nv), field(nl)[0])
            lm = field(nm)
            for c in range(2):
                out[at, pl.ds(c * LANES, LANES)] = lm[c] * (mid[c] - ((fb[c] - fa[c]) + dy[c]))

    ub0 = [ub0_s[:, pl.ds(c * LANES, LANES)] for c in range(2)]

    def one(pair, _):
        outs = [[], []]
        group = pl.ds(pl.multiple_of(pair * SUB, SUB), SUB)

        def beside(ref, n, *lead):
            return [
                jnp.broadcast_to(ref[(*lead, group, pl.ds(c * LANES, LANES))][n : n + 1], (SUB, LANES))
                for c in range(2)
            ]

        for h in range(2):
            f = pair * 2 + h
            cg = cg_ref[i * freqs + f]
            w = weight_ref[i * freqs + f]
            wr = w * ratio_ref[i * freqs + f]
            a2 = []
            for d in range(dirs):
                gc, gs = cg * tab_ref[sec, COS + 1 + d], cg * tab_ref[sec, SIN + 1 + d]
                ub, vb = tiles(ub_s), tiles(vb_s)
                vl = [0.5 * cur_ref[1, pl.ds(r * SUB, SUB), pl.ds(0, LANES)] for r in range(2)]
                land = [[m.astype(F32) for m in rw] for rw in tiles(land_ref)]
                t = tiles(x_ref, f, d)
                t = [[land[r][c] * t[r][c] for c in range(2)] for r in range(2)]
                lo, hi = beside(top_ref, h * dirs + d, 1), beside(bot_ref, h * dirs + d, 0)
                t = advance(g, t, gc, gs, ub, ub0, vb, vl, land, lo, hi)
                lo, hi = beside(at_s, h * dirs + d), beside(ab_s, h * dirs + d)
                t = advance(g, t, gc, gs, ub, ub0, vb, vl, land, lo, hi)
                a2.append(t)
            for r in range(2):
                for c in range(2):
                    here = (pl.ds(r * SUB, SUB), pl.ds(c * LANES, LANES))
                    v = [a2[d][r][c] for d in range(dirs)]
                    for d in range(dirs):
                        r_s[(d, *here)] += wr * v[d]
                    b_s[here] += w * ((v[0] + v[1]) + (v[2] + v[3]))
                    k = [k_s[(n, *here)] for n in range(dirs + 1)]
                    inside = [face_flux(k[d + 1], v[d], v[d + 1]) for d in range(dirs - 1)]
                    new_ref[(f, 1, *here)] = v[1] - (inside[1] - inside[0])
                    new_ref[(f, 2, *here)] = v[2] - (inside[2] - inside[1])
                    new_ref[(f, 0, *here)] = v[0] - (inside[0] - jnp.minimum(k[0], 0.0) * v[0])
                    new_ref[(f, 3, *here)] = v[3] - (jnp.maximum(k[4], 0.0) * v[3] - inside[2])
            k0, k4 = tiles(k_s, 0), tiles(k_s, dirs)
            outs[0].append([[jnp.minimum(k0[r][c], 0.0) * a2[0][r][c] for c in range(2)] for r in range(2)])
            outs[1].append([[jnp.maximum(k4[r][c], 0.0) * a2[3][r][c] for c in range(2)] for r in range(2)])
        for ref, ends in ((prev_ref, outs[0]), (next_ref, outs[1])):
            for c in range(2):
                ref[pair, :, pl.ds(c * LANES, LANES)] = pack_outer(
                    g, [ends[0][r][c] for r in range(2)], [ends[1][r][c] for r in range(2)]
                )
        return 0

    lax.fori_loop(0, freqs // 2, one, 0)

    @pl.when(i == blocks - 1)
    def _():
        cs = [tab_ref[sec, COS + n] for n in range(dirs + 2)]
        sn = [tab_ref[sec, SIN + n] for n in range(dirs + 2)]
        coef = (
            [1.0 + a * a for a in cs],
            [a * b for a, b in zip(sn, cs)],
            [1.0 + b * b for b in sn],
        )
        k = [tiles(k_s, n) for n in range(dirs + 1)]
        b = tiles(b_s)
        stress = []
        for n, co in enumerate(coef):
            total_s = [[None] * 2 for _ in range(2)]
            for r in range(2):
                for c in range(2):
                    here = (pl.ds(r * SUB, SUB), pl.ds(c * LANES, LANES))
                    acc = -0.5 * b[r][c] if n != 1 else jnp.zeros((SUB, LANES), F32)
                    for d in range(dirs):
                        q = (
                            co[d + 1]
                            + jnp.maximum(k[d + 1][r][c], 0.0) * (co[d + 2] - co[d + 1])
                            + jnp.minimum(k[d][r][c], 0.0) * (co[d + 1] - co[d])
                        )
                        acc = acc + q * r_s[(d, *here)]
                    total_s[r][c] = acc
            stress.append(total_s)
        zero = [jnp.zeros((SUB, LANES), F32)] * 2
        xx, xy, yy = stress
        dx = lambda t: half_diff(g.below(t, zero), g.above(t, zero))
        dy = lambda t: half_diff([g.right(r) for r in t], [g.left(r, 0.0) for r in t])
        for n, (p, q) in enumerate(((dx(xx), dy(xy)), (dx(xy), dy(yy)))):
            put_tiles(force_ref, [[-(p[r][c] + q[r][c]) for c in range(2)] for r in range(2)], n)
        for n, t in enumerate((xx, xy)):
            for c in range(2):
                brow_ref[0, pl.ds(n, 1), pl.ds(c * LANES, LANES)] = 0.5 * t[1][c][7:8, :]
                brow_ref[1, pl.ds(n, 1), pl.ds(c * LANES, LANES)] = -0.5 * t[0][c][0:1, :]


def join_kernel(e_ref, inp_ref, inn_ref, outp_ref, outn_ref, o_ref):
    g = Grid()
    j = pl.program_id(1)
    pairs = inp_ref.shape[0]

    def run(inner_ref, outer_ref, sign):
        def one(pair, _):
            for c in range(2):
                cc = pl.ds(c * LANES, LANES)
                inner = [inner_ref[pair, pl.ds(q * SUB, SUB), cc] for q in range(3)]
                both = unpack(g, inner, outer_ref[pair, :, cc])
                for h in range(2):
                    for r in range(2):
                        at = (pair * 2 + h, 0, pl.ds(r * SUB, SUB), cc)
                        o_ref[at] = e_ref[at] + sign * both[h][r]
            return 0

        lax.fori_loop(0, pairs, one, 0)

    @pl.when(j == 0)
    def _():
        run(inp_ref, outp_ref, 1.0)

    @pl.when(j == 1)
    def _():
        run(inn_ref, outn_ref, -1.0)


def per_device(sectors, points, action, currents, land_mask, group_speed, group_ratio, bin_weight):
    freqs, dirs, rows, cols = action.shape
    total = dirs * sectors
    table = jnp.asarray(angle_table(sectors, dirs))
    sec = lax.axis_index("dir").reshape(1).astype(jnp.int32)
    smem = pl.BlockSpec(memory_space=pltpu.SMEM)
    whole = lambda a: pl.BlockSpec(a.shape, lambda i: (0,) * a.ndim)
    fb = 10
    nb = freqs // fb
    combos = freqs * dirs
    f32 = lambda *s: jax.ShapeDtypeStruct(s, F32)
    vmem = lambda *s: pltpu.VMEM(s, F32)
    params = lambda: pltpu.CompilerParams(vmem_limit_bytes=24 * 2**20)

    flat = action.reshape(combos, rows // SUB, SUB, cols // LANES, LANES)
    flat = flat.transpose(0, 1, 3, 2, 4).reshape(combos * rows * cols // LANES, LANES)
    up_rows, dn_rows = pl.pallas_call(
        rows_kernel,
        grid=(nb,),
        in_specs=[
            pl.BlockSpec((fb * dirs * rows * cols // LANES, LANES), lambda i: (i, 0)),
            whole(currents),
            whole(land_mask),
        ],
        out_specs=[pl.BlockSpec((2, combos + SUB, cols), lambda i: (0, 0, 0))] * 2,
        out_shape=[f32(2, combos + SUB, cols)] * 2,
        compiler_params=params(),
        name="boundary_rows",
    )(flat, currents, land_mask)
    up = [(i, i + 1) for i in range(points - 1)]
    down = [(j, i) for i, j in up]
    top = lax.ppermute(up_rows, "pts", up)
    bot = lax.ppermute(dn_rows, "pts", down)

    in_prev, in_next = pl.pallas_call(
        functools.partial(ends_kernel, total),
        grid=(nb,),
        in_specs=[
            smem, smem, smem,
            pl.BlockSpec((fb, 1, rows, cols), lambda i: (i, 0, 0, 0)),
            pl.BlockSpec((fb, 1, rows, cols), lambda i: (i, dirs - 1, 0, 0)),
            whole(currents),
            whole(land_mask),
        ],
        out_specs=[pl.BlockSpec((fb // 2, 24, cols), lambda i: (i, 0, 0))] * 2,
        out_shape=[f32(freqs // 2, 24, cols)] * 2,
        scratch_shapes=[vmem(rows, cols), vmem(rows, cols), vmem(2, rows, cols)],
        compiler_params=params(),
        name="sector_ends",
    )(sec, table, group_speed, action, action, currents, land_mask)
    fwd = [(i, (i + 1) % sectors) for i in range(sectors)]
    back = [(j, i) for i, j in fwd]
    inner_from_prev = lax.ppermute(in_next, "dir", fwd)
    inner_from_next = lax.ppermute(in_prev, "dir", back)

    angles = table[lax.axis_index("dir")]
    cgc = (group_speed[:, None] * angles[None, COS + 1 : COS + 1 + dirs]).reshape(combos, 1)
    cgs = (group_speed[:, None] * angles[None, SIN + 1 : SIN + 1 + dirs]).reshape(combos, 1)
    cgc = jnp.broadcast_to(cgc, (combos, LANES))
    cgs = jnp.broadcast_to(cgs, (combos, LANES))
    cb = fb * dirs
    halo = pl.BlockSpec((2, cb, cols), lambda i: (0, i, 0))
    halo_fields = pl.BlockSpec((2, SUB, cols), lambda i: (0, combos // SUB, 0))
    part, out_prev, out_next, force, brow = pl.pallas_call(
        functools.partial(main_kernel, total),
        grid=(nb,),
        in_specs=[
            smem, smem, smem, smem, smem,
            pl.BlockSpec((fb, dirs, rows, cols), lambda i: (i, 0, 0, 0)),
            pl.BlockSpec((cb, LANES), lambda i: (i, 0)),
            pl.BlockSpec((cb, LANES), lambda i: (i, 0)),
            whole(currents),
            whole(land_mask),
            halo, halo, halo, halo, halo_fields, halo_fields,
        ],
        out_specs=[
            pl.BlockSpec((fb, dirs, rows, cols), lambda i: (i, 0, 0, 0)),
            pl.BlockSpec((fb // 2, SUB, cols), lambda i: (i, 0, 0)),
            pl.BlockSpec((fb // 2, SUB, cols), lambda i: (i, 0, 0)),
            pl.BlockSpec((2, rows, cols), lambda i: (0, 0, 0)),
            pl.BlockSpec((2, 2, cols), lambda i: (0, 0, 0)),
        ],
        out_shape=[
            f32(freqs, dirs, rows, cols),
            f32(freqs // 2, SUB, cols),
            f32(freqs // 2, SUB, cols),
            f32(2, rows, cols),
            f32(2, 2, cols),
        ],
        scratch_shapes=[
            vmem(rows, cols), vmem(SUB, cols), vmem(rows, cols), vmem(dirs + 1, rows, cols),
            vmem(9, SUB, cols), vmem(cb, cols), vmem(cb, cols),
            vmem(dirs, rows, cols), vmem(rows, cols),
        ],
        compiler_params=params(),
        name="transport",
    )(sec, table, group_speed, group_ratio, bin_weight, action, cgc, cgs, currents, land_mask,
      top, bot, up_rows, dn_rows, top, bot)

    from_above = lax.ppermute(brow[0], "pts", up)
    from_below = lax.ppermute(brow[1], "pts", down)
    outer_from_prev = lax.ppermute(out_next, "dir", fwd)
    outer_from_next = lax.ppermute(out_prev, "dir", back)
    force = jnp.concatenate(
        [force[:, :1] + from_above[:, None], force[:, 1:-1], force[:, -1:] + from_below[:, None]], axis=1
    )
    half = sectors // 2
    force = force + lax.ppermute(force, "dir", [(i, (i + half) % sectors) for i in range(sectors)])
    near = [
        lax.ppermute(
            force, "dir", [(i, i // half * half + (i % half + s) % half) for i in range(sectors)]
        )
        for s in range(1, half)
    ]
    force = (force + near[1]) + (near[0] + near[2])

    new_action = pl.pallas_call(
        join_kernel,
        grid=(nb, 2),
        in_specs=[
            pl.BlockSpec((fb, 1, rows, cols), lambda i, j: (i, j * (dirs - 1), 0, 0)),
            pl.BlockSpec((fb // 2, 24, cols), lambda i, j: (i, 0, 0)),
            pl.BlockSpec((fb // 2, 24, cols), lambda i, j: (i, 0, 0)),
            pl.BlockSpec((fb // 2, SUB, cols), lambda i, j: (i, 0, 0)),
            pl.BlockSpec((fb // 2, SUB, cols), lambda i, j: (i, 0, 0)),
        ],
        out_specs=pl.BlockSpec((fb, 1, rows, cols), lambda i, j: (i, j * (dirs - 1), 0, 0)),
        out_shape=f32(freqs, dirs, rows, cols),
        input_output_aliases={0: 0},
        compiler_params=params(),
        name="join_sectors",
    )(part, inner_from_prev, inner_from_next, outer_from_prev, outer_from_next)
    return new_action, force


def solution(mesh):
    in_specs = (P(None, "dir", "pts", None), P(None, "pts", None), P("pts", None), P(), P(), P())
    out_specs = (P(None, "dir", "pts", None), P(None, "pts", None))
    return jax.shard_map(
        functools.partial(per_device, mesh.shape["dir"], mesh.shape["pts"]),
        mesh=mesh, in_specs=in_specs, out_specs=out_specs, check_vma=False,
    )
```

```python
import math
import functools

import numpy as np
import jax
import jax.numpy as jnp
from jax import lax
from jax.sharding import PartitionSpec as P
from jax.experimental import pallas as pl
from jax.experimental.pallas import tpu as pltpu


F32 = jnp.float32
LANES = 128
SUB = 8


def iota_masks():
    s = lax.broadcasted_iota(jnp.int32, (SUB, LANES), 0)
    l = lax.broadcasted_iota(jnp.int32, (SUB, LANES), 1)
    return s, l


def roll(x, shift, axis):
    return pltpu.roll(x, shift, axis)


class Grid:
    def __init__(self):
        s, l = iota_masks()
        self.s = s
        self.first_row = s == 0
        self.last_row = s == SUB - 1
        self.first_col = l == 0
        self.last_col = l == LANES - 1

    def below(self, t, hi):
        n, m = len(t), len(t[0])
        moved = [[roll(t[r][c], SUB - 1, 0) for c in range(m)] for r in range(n)]
        return [
            [
                jnp.where(self.last_row, moved[r + 1][c] if r + 1 < n else hi[c], moved[r][c])
                for c in range(m)
            ]
            for r in range(n)
        ]

    def above(self, t, lo):
        n, m = len(t), len(t[0])
        moved = [[roll(t[r][c], 1, 0) for c in range(m)] for r in range(n)]
        return [
            [
                jnp.where(self.first_row, moved[r - 1][c] if r > 0 else lo[c], moved[r][c])
                for c in range(m)
            ]
            for r in range(n)
        ]

    def right(self, row):
        m = len(row)
        moved = [roll(v, LANES - 1, 1) for v in row]
        return [
            jnp.where(self.last_col, moved[c + 1] if c + 1 < m else 0.0, moved[c]) for c in range(m)
        ]

    def left(self, row, start):
        m = len(row)
        moved = [roll(v, 1, 1) for v in row]
        return [
            jnp.where(self.first_col, moved[c - 1] if c > 0 else start, moved[c]) for c in range(m)
        ]


def face_flux(c, behind, in_front):
    return c * jnp.where(c > 0.0, behind, in_front)


def col_change(g, row, gs, vb, vl):
    right = g.right(row)
    flux = [face_flux(gs + vb[c], row[c], right[c]) for c in range(len(row))]
    edge = jnp.minimum(gs + vl, 0.0) * row[0]
    left = g.left(flux, edge)
    return [flux[c] - left[c] for c in range(len(row))]


def advance(g, t, gc, gs, ub, vb, vl, land, start, hi):
    n, m = len(t), len(t[0])
    ahead = g.below(t, hi)
    flux = [[face_flux(gc + ub[r][c], t[r][c], ahead[r][c]) for c in range(m)] for r in range(n)]
    before = g.above(flux, start)
    out = []
    for r in range(n):
        dy = col_change(g, t[r], gs, vb[r], vl[r])
        out.append(
            [land[r][c] * (t[r][c] - ((flux[r][c] - before[r][c]) + dy[c])) for c in range(m)]
        )
    return out


def tiles(ref, *lead):
    rows, cols = ref.shape[-2] // SUB, ref.shape[-1] // LANES
    return [
        [ref[(*lead, pl.ds(r * SUB, SUB), pl.ds(c * LANES, LANES))] for c in range(cols)]
        for r in range(rows)
    ]


def put_tiles(ref, t, *lead):
    for r, row in enumerate(t):
        for c, v in enumerate(row):
            ref[(*lead, pl.ds(r * SUB, SUB), pl.ds(c * LANES, LANES))] = v


def spread_row(ref, cols, *index):
    *lead, row = index
    return [
        jnp.broadcast_to(ref[(*lead, pl.ds(row, 1), pl.ds(c * LANES, LANES))], (SUB, LANES))
        for c in range(cols)
    ]


def turning(shears, sine, cosine, total_dirs):
    ux, uy, vx, vy = shears
    scale = total_dirs / (2.0 * math.pi)
    return [
        [
            scale
            * (
                sine * cosine * (ux[r][c] - vy[r][c])
                + sine * sine * uy[r][c]
                - cosine * cosine * vx[r][c]
            )
            for c in range(len(ux[0]))
        ]
        for r in range(len(ux))
    ]


def half_sum(a, b):
    return [[0.5 * (x + y) for x, y in zip(p, q)] for p, q in zip(a, b)]


def half_diff(a, b):
    return [[0.5 * (x - y) for x, y in zip(p, q)] for p, q in zip(a, b)]


def shears_of(g, u, v, u_lo, u_hi, v_lo, v_hi):
    ux = half_diff(g.below(u, u_hi), g.above(u, u_lo))
    vx = half_diff(g.below(v, v_hi), g.above(v, v_lo))
    uy = half_diff([g.right(r) for r in u], [g.left(r, 0.0) for r in u])
    vy = half_diff([g.right(r) for r in v], [g.left(r, 0.0) for r in v])
    return ux, uy, vx, vy


COS, SIN, FCOS, FSIN = 0, 6, 12, 17
TABLE = 22


def angle_table(sectors, per):
    total = sectors * per
    step = 2.0 * math.pi / total
    out = np.zeros((sectors, TABLE), np.float64)
    for k in range(sectors):
        d = np.arange(-1, per + 1) + k * per
        out[k, COS : COS + per + 2] = np.cos(d * step)
        out[k, SIN : SIN + per + 2] = np.sin(d * step)
        face = (np.arange(per + 1) + k * per - 0.5) * step
        out[k, FCOS : FCOS + per + 1] = np.cos(face)
        out[k, FSIN : FSIN + per + 1] = np.sin(face)
    return out.astype(np.float32)


HALO = 3


def rows_kernel(x_ref, fld_ref, up_ref, dn_ref):
    last = up_ref.shape[1] - SUB
    sides = ((up_ref, range(16 - HALO, 16)), (dn_ref, range(HALO)))
    for ref, rows in sides:
        for k, row in enumerate(rows):
            ref[k, pl.ds(last, SUB), :] = jnp.zeros((SUB, 2 * LANES), F32)
            for n in range(3):
                ref[k, pl.ds(last + n, 1), :] = fld_ref[n, pl.ds(row, 1), :]

    def one(q, _):
        at = pl.multiple_of(q * SUB, SUB)
        for ref, rows in sides:
            for k, row in enumerate(rows):
                for c in range(2):
                    start = at * 32 + (row // SUB * 2 + c) * SUB + row % SUB
                    v = x_ref[pl.ds(start, SUB, stride=32), :]
                    land = spread_row(fld_ref, 2, 2, row)[c]
                    ref[k, pl.ds(at, SUB), pl.ds(c * LANES, LANES)] = v * land
        return 0

    lax.fori_loop(0, last // SUB, one, 0)


def pack_inner(g, a, b):
    low2 = g.s < 6
    first = jnp.where(low2, roll(a[0], 6, 0), roll(a[1], 6, 0))
    mid = jnp.where(g.s < 4, roll(a[1], 6, 0), roll(b[0], 2, 0))
    last = jnp.where(g.s < 2, roll(b[0], 2, 0), roll(b[1], 2, 0))
    return first, mid, last


def pack_outer(g, a, b):
    one = jnp.where(g.s < 2, a[0], roll(a[1], 4, 0))
    two = jnp.where(g.s < 6, roll(b[0], 4, 0), b[1])
    return jnp.where(g.s < 4, one, two)


def unpack(g, inner, outer):
    a, b, c = inner
    a2, b2, b6, c6, o4 = roll(a, 2, 0), roll(b, 2, 0), roll(b, 6, 0), roll(c, 6, 0), roll(outer, 4, 0)
    low2, low6 = g.s < 2, g.s < 6
    one = [jnp.where(low2, outer, a2), jnp.where(low2, a2, jnp.where(low6, b2, o4))]
    two = [jnp.where(low2, o4, jnp.where(low6, b6, c6)), jnp.where(low6, c6, outer)]
    return one, two


def ends_kernel(total, sec_ref, tab_ref, cg_ref, x_ref, cur_ref,
                prev_ref, next_ref, ub_s, vb_s, k_s):
    g = Grid()
    sec = sec_ref[0]
    freqs = x_ref.shape[0]
    zero = [jnp.zeros((SUB, LANES), F32)] * 2

    u, v = tiles(cur_ref, 0), tiles(cur_ref, 1)
    put_tiles(ub_s, half_sum(u, g.below(u, zero)))
    put_tiles(vb_s, half_sum(v, [g.right(r) for r in v]))
    sh = shears_of(g, u, v, zero, zero, zero, zero)
    for n, f in ((0, 0), (1, 4)):
        put_tiles(k_s, turning(sh, tab_ref[sec, FSIN + f], tab_ref[sec, FCOS + f], total), n)

    def one(pair, _):
        for n, (out_ref, d) in enumerate(((prev_ref, 0), (next_ref, 3))):
            ends = []
            for h in range(2):
                f = pair * 2 + h
                cg = cg_ref[f]
                gc, gs = cg * tab_ref[sec, COS + 1 + d], cg * tab_ref[sec, SIN + 1 + d]
                ub, vb = tiles(ub_s), tiles(vb_s)
                vl = [0.5 * cur_ref[1, pl.ds(r * SUB, SUB), pl.ds(0, LANES)] for r in range(2)]
                land = tiles(cur_ref, 2)
                t = tiles(x_ref, f, d)
                t = [[land[r][c] * t[r][c] for c in range(2)] for r in range(2)]
                for _ in range(2):
                    t = advance(g, t, gc, gs, ub, vb, vl, land, zero, zero)
                k = tiles(k_s, n)
                limit = jnp.minimum if d == 0 else jnp.maximum
                ends.append([[limit(k[r][c], 0.0) * t[r][c] for c in range(2)] for r in range(2)])
            for c in range(2):
                got = pack_inner(g, [ends[0][r][c] for r in range(2)], [ends[1][r][c] for r in range(2)])
                for q in range(3):
                    out_ref[pair, pl.ds(q * SUB, SUB), pl.ds(c * LANES, LANES)] = got[q]
        return 0

    lax.fori_loop(0, freqs // 2, one, 0)


FACE, VROW, VLEFT, LAND, SIDE = 0, 4, 7, 10, 13


def column_rows(g, rows, field, gc, gs):
    m = range(2)
    flux = [
        [face_flux(gc + field(FACE + i)[c], rows[i][c], rows[i + 1][c]) for c in m] for i in range(4)
    ]
    once = []
    for i in range(3):
        dy = col_change(g, rows[i + 1], gs, field(VROW + i), field(VLEFT + i)[0])
        land = field(LAND + i)
        once.append([land[c] * (rows[i + 1][c] - ((flux[i + 1][c] - flux[i][c]) + dy[c])) for c in m])
    again = [
        [face_flux(gc + field(FACE + 1 + i)[c], once[i][c], once[i + 1][c]) for c in m] for i in range(2)
    ]
    dy = col_change(g, once[1], gs, field(VROW + 1), field(VLEFT + 1)[0])
    land = field(LAND + 1)
    twice = [land[c] * (once[1][c] - ((again[1][c] - again[0][c]) + dy[c])) for c in m]
    return flux, again, once, twice


def stress_of(co, k, r, b, n, dirs):
    acc = -0.5 * b if n != 1 else jnp.zeros((SUB, LANES), F32)
    for d in range(dirs):
        q = (
            co[d + 1]
            + jnp.maximum(k[d + 1], 0.0) * (co[d + 2] - co[d + 1])
            + jnp.minimum(k[d], 0.0) * (co[d + 1] - co[d])
        )
        acc = acc + q * r[d]
    return acc


def main_kernel(total, sec_ref, tab_ref, cg_ref, ratio_ref, weight_ref,
                x_ref, cur_ref, top_ref, bot_ref, ownup_ref, owndn_ref,
                part_ref, e0_ref, e3_ref, prev_ref, next_ref, force_ref,
                new_ref, sem, ub_s, vb_s, k_s, fld_s, ke_s, st_s, r_s, b_s, re_s, be_s):
    g = Grid()
    chunks = sem.shape[0]
    sec = sec_ref[0]
    freqs = x_ref.shape[0]
    dirs = x_ref.shape[1]

    last = freqs * dirs
    u, v = tiles(cur_ref, 0), tiles(cur_ref, 1)

    def beside_fields(n):
        above = [spread_row(top_ref, 2, q, last + n) for q in range(HALO)]
        below = [spread_row(bot_ref, 2, q, last + n) for q in range(HALO)]
        own = [spread_row(cur_ref, 2, n, q) for q in (0, 1, 14, 15)]
        return above + own[:2], own[2:] + below

    us, vs, ls = (beside_fields(n) for n in range(3))
    put_tiles(ub_s, half_sum(u, g.below(u, us[1][2])))
    put_tiles(vb_s, half_sum(v, [g.right(r) for r in v]))
    for side in range(2):
        for q in range(4):
            put_tiles(fld_s, half_sum([us[side][q]], [us[side][q + 1]]), side, FACE + q)
        for q in range(3):
            vv = vs[side][q + 1]
            put_tiles(fld_s, half_sum([vv], [g.right(vv)]), side, VROW + q)
            put_tiles(fld_s, [[0.5 * w for w in vv]], side, VLEFT + q)
            put_tiles(fld_s, [ls[side][q + 1]], side, LAND + q)
        edge = (
            half_diff([us[side][3]], [us[side][1]]),
            half_diff([g.right(us[side][2])], [g.left(us[side][2], 0.0)]),
            half_diff([vs[side][3]], [vs[side][1]]),
            half_diff([g.right(vs[side][2])], [g.left(vs[side][2], 0.0)]),
        )
        for f in range(dirs + 1):
            k = turning(edge, tab_ref[sec, FSIN + f], tab_ref[sec, FCOS + f], total)
            put_tiles(ke_s, k, side, f)
    sh = shears_of(g, u, v, us[0][2], us[1][2], vs[0][2], vs[1][2])
    for f in range(dirs + 1):
        put_tiles(k_s, turning(sh, tab_ref[sec, FSIN + f], tab_ref[sec, FCOS + f], total), f)
    for ref in (r_s, b_s, re_s, be_s):
        ref[...] = jnp.zeros_like(ref)

    def by_direction(n):
        out = jnp.zeros((SUB, LANES), F32)
        for d in range(dirs):
            out = jnp.where(g.s % dirs == d, tab_ref[sec, n + 1 + d], out)
        return out

    cos_rows, sin_rows = by_direction(COS), by_direction(SIN)

    def beside_rows(q, _):
        at = pl.ds(pl.multiple_of(q * SUB, SUB), SUB)
        pair = lambda a, b: jnp.where(g.s < dirs, a, b)
        f = q * 2
        cg = pair(cg_ref[f], cg_ref[f + 1])
        gc, gs = cg * cos_rows, cg * sin_rows
        w = pair(weight_ref[f], weight_ref[f + 1])
        wr = w * pair(ratio_ref[f], ratio_ref[f + 1])
        row = lambda ref, n: [ref[n, at, pl.ds(c * LANES, LANES)] for c in range(2)]
        above = [row(top_ref, n) for n in range(HALO)]
        below = [row(bot_ref, n) for n in range(HALO)]
        for side, rows in (
            (0, above + [row(owndn_ref, 0), row(owndn_ref, 1)]),
            (1, [row(ownup_ref, 1), row(ownup_ref, 2)] + below),
        ):
            field = lambda n: [fld_s[side, n, :, pl.ds(c * LANES, LANES)] for c in range(2)]
            flux, again, once, twice = column_rows(g, rows, field, gc, gs)
            for c in range(2):
                cc = pl.ds(c * LANES, LANES)
                if side == 0:
                    st_s[0, at, cc] = flux[2][c]
                    st_s[1, at, cc] = again[1][c]
                else:
                    st_s[2, at, cc] = once[1][c]
                re_s[side, :, cc] += wr * twice[c]
                be_s[side, :, cc] += w * twice[c]
        return 0

    lax.fori_loop(0, freqs * dirs // SUB, beside_rows, 0)

    def one(pair, _):
        outs = [[], []]
        group = pl.ds(pl.multiple_of(pair * SUB, SUB), SUB)

        def beside(ref, n, *lead):
            return [
                jnp.broadcast_to(ref[(*lead, group, pl.ds(c * LANES, LANES))][n : n + 1], (SUB, LANES))
                for c in range(2)
            ]

        for h in range(2):
            f = pair * 2 + h
            cg = cg_ref[f]
            w = weight_ref[f]
            wr = w * ratio_ref[f]
            a2 = []
            for d in range(dirs):
                gc, gs = cg * tab_ref[sec, COS + 1 + d], cg * tab_ref[sec, SIN + 1 + d]
                ub, vb = tiles(ub_s), tiles(vb_s)
                vl = [0.5 * cur_ref[1, pl.ds(r * SUB, SUB), pl.ds(0, LANES)] for r in range(2)]
                land = tiles(cur_ref, 2)
                t = tiles(x_ref, f, d)
                t = [[land[r][c] * t[r][c] for c in range(2)] for r in range(2)]
                n = h * dirs + d
                t = advance(g, t, gc, gs, ub, vb, vl, land, beside(st_s, n, 0), beside(bot_ref, n, 0))
                t = advance(g, t, gc, gs, ub, vb, vl, land, beside(st_s, n, 1), beside(st_s, n, 2))
                a2.append(t)
            for r in range(2):
                for c in range(2):
                    here = (pl.ds(r * SUB, SUB), pl.ds(c * LANES, LANES))
                    v = [a2[d][r][c] for d in range(dirs)]
                    for d in range(dirs):
                        r_s[(d, *here)] += wr * v[d]
                    b_s[here] += w * ((v[0] + v[1]) + (v[2] + v[3]))
                    k = [k_s[(n, *here)] for n in range(dirs + 1)]
                    inside = [face_flux(k[d + 1], v[d], v[d + 1]) for d in range(dirs - 1)]
                    new_ref[(f, 0, *here)] = v[1] - (inside[1] - inside[0])
                    new_ref[(f, 1, *here)] = v[2] - (inside[2] - inside[1])
                    e0_ref[(f, *here)] = v[0] - (inside[0] - jnp.minimum(k[0], 0.0) * v[0])
                    e3_ref[(f, *here)] = v[3] - (jnp.maximum(k[4], 0.0) * v[3] - inside[2])
            k0, k4 = tiles(k_s, 0), tiles(k_s, dirs)
            outs[0].append([[jnp.minimum(k0[r][c], 0.0) * a2[0][r][c] for c in range(2)] for r in range(2)])
            outs[1].append([[jnp.maximum(k4[r][c], 0.0) * a2[3][r][c] for c in range(2)] for r in range(2)])
        for ref, ends in ((prev_ref, outs[0]), (next_ref, outs[1])):
            for c in range(2):
                ref[pair, :, pl.ds(c * LANES, LANES)] = pack_outer(
                    g, [ends[0][r][c] for r in range(2)], [ends[1][r][c] for r in range(2)]
                )
        return 0

    per = freqs // chunks

    def put(q):
        span = pl.ds(q * per, per)
        return pltpu.make_async_copy(
            new_ref.at[span], part_ref.at[span, pl.ds(1, dirs - 2)], sem.at[q]
        )

    def chunk(q, _):
        lax.fori_loop(q * (per // 2), (q + 1) * (per // 2), one, 0)
        put(q).start()
        return 0

    lax.fori_loop(0, chunks, chunk, 0)
    cs = [tab_ref[sec, COS + n] for n in range(dirs + 2)]
    sn = [tab_ref[sec, SIN + n] for n in range(dirs + 2)]
    coef = (
        [1.0 + a * a for a in cs],
        [a * b for a, b in zip(sn, cs)],
        [1.0 + b * b for b in sn],
    )
    stress, edges = [], []
    for n, co in enumerate(coef):
        now = []
        for r in range(2):
            now.append([])
            for c in range(2):
                here = (pl.ds(r * SUB, SUB), pl.ds(c * LANES, LANES))
                k = [k_s[(m, *here)] for m in range(dirs + 1)]
                now[r].append(
                    stress_of(co, k, [r_s[(d, *here)] for d in range(dirs)], b_s[here], n, dirs)
                )
        stress.append(now)
        both = []
        for side in range(2):
            both.append([])
            for c in range(2):
                cc = pl.ds(c * LANES, LANES)
                rr, bb = re_s[side, :, cc], be_s[side, :, cc]
                spread = lambda v: jnp.broadcast_to(v, (SUB, LANES))
                k = [ke_s[side, m, :, cc] for m in range(dirs + 1)]
                rd = [spread(rr[d : d + 1] + rr[d + dirs : d + dirs + 1]) for d in range(dirs)]
                both[side].append(
                    stress_of(co, k, rd, spread(jnp.sum(bb, axis=0, keepdims=True)), n, dirs)
                )
        edges.append(both)
    xx, xy, yy = stress
    dx = lambda t, e: half_diff(g.below(t, e[1]), g.above(t, e[0]))
    dy = lambda t: half_diff([g.right(r) for r in t], [g.left(r, 0.0) for r in t])
    for n, (p, q) in enumerate(((dx(xx, edges[0]), dy(xy)), (dx(xy, edges[1]), dy(yy)))):
        put_tiles(force_ref, [[-(p[r][c] + q[r][c]) for c in range(2)] for r in range(2)], n)

    def done(q, _):
        put(q).wait()
        return 0

    lax.fori_loop(0, chunks, done, 0)


def join_kernel(e0_ref, e3_ref, inp_ref, inn_ref, outp_ref, outn_ref, part_ref, o_ref, buf, sem):
    g = Grid()
    pairs = inp_ref.shape[0]
    dirs = o_ref.shape[1]
    parts = 5
    step = pairs // parts

    def put(q, n, d):
        span = pl.ds(q * step * 2, step * 2)
        return pltpu.make_async_copy(buf.at[n, span], o_ref.at[span, d], sem.at[q, n])

    for q in range(parts):
        for n, (e_ref, inner_ref, outer_ref, sign, d) in enumerate(
            ((e0_ref, inp_ref, outp_ref, 1.0, 0), (e3_ref, inn_ref, outn_ref, -1.0, dirs - 1))
        ):
            def one(pair, _):
                for c in range(2):
                    cc = pl.ds(c * LANES, LANES)
                    inner = [inner_ref[pair, pl.ds(k * SUB, SUB), cc] for k in range(3)]
                    both = unpack(g, inner, outer_ref[pair, :, cc])
                    for h in range(2):
                        for r in range(2):
                            at = (pair * 2 + h, pl.ds(r * SUB, SUB), cc)
                            buf[(n, *at)] = e_ref[at] + sign * both[h][r]
                return 0

            lax.fori_loop(q * step, (q + 1) * step, one, 0)
            put(q, n, d).start()
    for q in range(parts):
        put(q, 0, 0).wait()
        put(q, 1, dirs - 1).wait()


def per_device(sectors, points, action, currents, land_mask, group_speed, group_ratio, bin_weight):
    freqs, dirs, rows, cols = action.shape
    total = dirs * sectors
    table = jnp.asarray(angle_table(sectors, dirs))
    sec = lax.axis_index("dir").reshape(1).astype(jnp.int32)
    smem = pl.BlockSpec(memory_space=pltpu.SMEM)
    combos = freqs * dirs
    f32 = lambda *s: jax.ShapeDtypeStruct(s, F32)

    def send(value, axis, pairs):
        return lax.ppermute(value, axis, pairs)

    vmem = lambda *s: pltpu.VMEM(s, F32)
    params = lambda: pltpu.CompilerParams(vmem_limit_bytes=24 * 2**20)

    fields = jnp.concatenate([currents, land_mask.astype(F32)[None]])
    flat = action.reshape(combos, rows // SUB, SUB, cols // LANES, LANES)
    flat = flat.transpose(0, 1, 3, 2, 4).reshape(combos * rows * cols // LANES, LANES)
    vm = pl.BlockSpec(memory_space=pltpu.VMEM)
    hbm = pl.BlockSpec(memory_space=pl.ANY)
    up_rows, dn_rows = pl.pallas_call(
        rows_kernel,
        in_specs=[vm, vm],
        out_specs=[vm, vm],
        out_shape=[f32(HALO, combos + SUB, cols)] * 2,
        compiler_params=params(),
        name="boundary_rows",
    )(flat, fields)
    up = [(i, i + 1) for i in range(points - 1)]
    down = [(j, i) for i, j in up]
    top = send(up_rows, "pts", up)
    bot = send(dn_rows, "pts", down)

    in_prev, in_next = pl.pallas_call(
        functools.partial(ends_kernel, total),
        in_specs=[smem, smem, smem, vm, vm],
        out_specs=[vm, vm],
        out_shape=[f32(freqs // 2, 24, cols)] * 2,
        scratch_shapes=[vmem(rows, cols), vmem(rows, cols), vmem(2, rows, cols)],
        compiler_params=params(),
        name="sector_ends",
    )(sec, table, group_speed, action, fields)
    fwd = [(i, (i + 1) % sectors) for i in range(sectors)]
    back = [(j, i) for i, j in fwd]
    inner_from_prev = send(in_next, "dir", fwd)
    inner_from_next = send(in_prev, "dir", back)

    part, e0, e3, out_prev, out_next, force = pl.pallas_call(
        functools.partial(main_kernel, total),
        in_specs=[smem] * 5 + [vm] * 6,
        out_specs=[hbm, vm, vm, vm, vm, vm],
        out_shape=[
            f32(freqs, dirs, rows, cols),
            f32(freqs, rows, cols),
            f32(freqs, rows, cols),
            f32(freqs // 2, SUB, cols),
            f32(freqs // 2, SUB, cols),
            f32(2, rows, cols),
        ],
        scratch_shapes=[
            vmem(freqs, dirs - 2, rows, cols), pltpu.SemaphoreType.DMA((5,)),
            vmem(rows, cols), vmem(rows, cols), vmem(dirs + 1, rows, cols),
            vmem(2, SIDE, SUB, cols), vmem(2, dirs + 1, SUB, cols), vmem(3, combos, cols),
            vmem(dirs, rows, cols), vmem(rows, cols), vmem(2, SUB, cols), vmem(2, SUB, cols),
        ],
        compiler_params=params(),
        name="transport",
    )(sec, table, group_speed, group_ratio, bin_weight, action, fields,
      top, bot, up_rows, dn_rows)

    outer_from_prev = send(out_next, "dir", fwd)
    outer_from_next = send(out_prev, "dir", back)
    half = sectors // 2
    force = force + send(force, "dir", [(i, (i + half) % sectors) for i in range(sectors)])
    near = [
        send(force, "dir",
             [(i, i // half * half + (i % half + s) % half) for i in range(sectors)])
        for s in range(1, half)
    ]
    force = (force + near[1]) + (near[0] + near[2])

    new_action = pl.pallas_call(
        join_kernel,
        in_specs=[vm] * 6 + [hbm],
        out_specs=hbm,
        out_shape=f32(freqs, dirs, rows, cols),
        input_output_aliases={6: 0},
        scratch_shapes=[vmem(2, freqs, rows, cols), pltpu.SemaphoreType.DMA((5, 2))],
        compiler_params=params(),
        name="join_sectors",
    )(e0, e3, inner_from_prev, inner_from_next, outer_from_prev, outer_from_next, part)
    return new_action, force


def solution(mesh):
    in_specs = (P(None, "dir", "pts", None), P(None, "pts", None), P("pts", None), P(), P(), P())
    out_specs = (P(None, "dir", "pts", None), P(None, "pts", None))

    def body(*args):
        return per_device(mesh.shape["dir"], mesh.shape["pts"], *args)

    return jax.shard_map(body, mesh=mesh, in_specs=in_specs, out_specs=out_specs, check_vma=False)
```

```python
import math
import functools

import numpy as np
import jax
import jax.numpy as jnp
from jax import lax
from jax.sharding import PartitionSpec as P
from jax.experimental import pallas as pl
from jax.experimental.pallas import tpu as pltpu


F32 = jnp.float32
LANES = 128
SUB = 8


def iota_masks():
    s = lax.broadcasted_iota(jnp.int32, (SUB, LANES), 0)
    l = lax.broadcasted_iota(jnp.int32, (SUB, LANES), 1)
    return s, l


def roll(x, shift, axis):
    return pltpu.roll(x, shift, axis)


class Grid:
    def __init__(self):
        s, l = iota_masks()
        self.s = s
        self.first_row = s == 0
        self.last_row = s == SUB - 1
        self.first_col = l == 0
        self.last_col = l == LANES - 1

    def below(self, t, hi):
        n, m = len(t), len(t[0])
        moved = [[roll(t[r][c], SUB - 1, 0) for c in range(m)] for r in range(n)]
        return [
            [
                jnp.where(self.last_row, moved[r + 1][c] if r + 1 < n else hi[c], moved[r][c])
                for c in range(m)
            ]
            for r in range(n)
        ]

    def above(self, t, lo):
        n, m = len(t), len(t[0])
        moved = [[roll(t[r][c], 1, 0) for c in range(m)] for r in range(n)]
        return [
            [
                jnp.where(self.first_row, moved[r - 1][c] if r > 0 else lo[c], moved[r][c])
                for c in range(m)
            ]
            for r in range(n)
        ]

    def right(self, row):
        m = len(row)
        moved = [roll(v, LANES - 1, 1) for v in row]
        return [
            jnp.where(self.last_col, moved[c + 1] if c + 1 < m else 0.0, moved[c]) for c in range(m)
        ]

    def left(self, row, start):
        m = len(row)
        moved = [roll(v, 1, 1) for v in row]
        return [
            jnp.where(self.first_col, moved[c - 1] if c > 0 else start, moved[c]) for c in range(m)
        ]


def face_flux(c, behind, in_front):
    return c * jnp.where(c > 0.0, behind, in_front)


def col_change(g, row, gs, vb, vl):
    right = g.right(row)
    flux = [face_flux(gs + vb[c], row[c], right[c]) for c in range(len(row))]
    edge = jnp.minimum(gs + vl, 0.0) * row[0]
    left = g.left(flux, edge)
    return [flux[c] - left[c] for c in range(len(row))]


def advance(g, t, right, left, gc, gs, ub, vb, vl, land, start, hi):
    n, m = len(t), len(t[0])
    ahead = g.below(t, hi)
    flux = [[face_flux(gc + ub[r][c], t[r][c], ahead[r][c]) for c in range(m)] for r in range(n)]
    before = g.above(flux, start)
    out = []
    for r in range(n):
        out.append([])
        for c in range(m):
            dy = face_flux(gs + vb[r][c], t[r][c], right[r][c]) - face_flux(
                gs + vl[r][c], left[r][c], t[r][c]
            )
            out[r].append(land[r][c] * (t[r][c] - ((flux[r][c] - before[r][c]) + dy)))
    return out


def shift_matrix(cols):
    at, to = np.arange(cols)[:, None], np.arange(cols)[None, :]
    both = np.concatenate([at == to + 1, at == to - 1], axis=1).astype(np.float32)
    return jnp.asarray(np.concatenate([both, both], axis=0), jnp.bfloat16)


def put_halves(ref, t, slot, n):
    cols = len(t[0]) * LANES
    at = pl.ds(n * 2 * SUB, 2 * SUB)
    for c in range(len(t[0])):
        v = jnp.concatenate([t[0][c], t[1][c]], axis=0)
        high = v.astype(jnp.bfloat16)
        low = (v - high.astype(F32)).astype(jnp.bfloat16)
        ref[slot, at, pl.ds(c * LANES, LANES)] = high
        ref[slot, at, pl.ds(cols + c * LANES, LANES)] = low


def block_of(ref, slot, n, first=0):
    return [
        [
            ref[slot, pl.ds((n * 2 + r) * SUB, SUB), pl.ds((first + c) * LANES, LANES)]
            for c in range(2)
        ]
        for r in range(2)
    ]


def put_block(ref, t, slot, n):
    for r in range(2):
        for c in range(2):
            ref[slot, pl.ds((n * 2 + r) * SUB, SUB), pl.ds(c * LANES, LANES)] = t[r][c]


class Substeps:
    def __init__(self, g, dirs, speeds, x_ref, cur_ref, mat_ref, ub_s, vb_s, vl_s, scratch):
        self.g, self.dirs, self.speeds = g, dirs, speeds
        self.x_ref, self.cur_ref, self.mat_ref = x_ref, cur_ref, mat_ref
        self.ub_s, self.vb_s, self.vl_s = ub_s, vb_s, vl_s
        self.t0, self.t1, self.h0, self.h1, self.y0, self.y1 = scratch
        self.members = [(h, d) for h in range(2) for d in dirs]

    def load(self, pair, slot):
        land = tiles(self.cur_ref, 2)
        for n, (h, d) in enumerate(self.members):
            x = tiles(self.x_ref, pair * 2 + h, d)
            t = [[land[r][c] * x[r][c] for c in range(2)] for r in range(2)]
            put_block(self.t0, t, slot, n)
            put_halves(self.h0, t, slot, n)
        self.y0[slot] = jnp.dot(self.h0[slot], self.mat_ref[...], preferred_element_type=F32)

    def step(self, pair, slot, n, t_ref, y_ref, start, hi):
        h, d = self.members[n]
        gc, gs = self.speeds(pair * 2 + h, d)
        return advance(
            self.g, block_of(t_ref, slot, n), block_of(y_ref, slot, n), block_of(y_ref, slot, n, 2),
            gc, gs, tiles(self.ub_s), tiles(self.vb_s), tiles(self.vl_s), tiles(self.cur_ref, 2),
            start, hi,
        )

    def first(self, pair, slot, edges):
        for n in range(len(self.members)):
            t = self.step(pair, slot, n, self.t0, self.y0, *edges(pair, n, 0))
            put_block(self.t1, t, slot, n)
            put_halves(self.h1, t, slot, n)
        self.y1[slot] = jnp.dot(self.h1[slot], self.mat_ref[...], preferred_element_type=F32)

    def second(self, pair, slot, edges, n):
        return self.step(pair, slot, n, self.t1, self.y1, *edges(pair, n, 1))


def substep_scratch(members, cols):
    rows = members * 2 * SUB
    return [
        pltpu.VMEM((2, rows, cols), F32),
        pltpu.VMEM((2, rows, cols), F32),
        pltpu.VMEM((2, rows, 2 * cols), jnp.bfloat16),
        pltpu.VMEM((2, rows, 2 * cols), jnp.bfloat16),
        pltpu.VMEM((2, rows, 2 * cols), F32),
        pltpu.VMEM((2, rows, 2 * cols), F32),
    ]


def tiles(ref, *lead):
    rows, cols = ref.shape[-2] // SUB, ref.shape[-1] // LANES
    return [
        [ref[(*lead, pl.ds(r * SUB, SUB), pl.ds(c * LANES, LANES))] for c in range(cols)]
        for r in range(rows)
    ]


def put_tiles(ref, t, *lead):
    for r, row in enumerate(t):
        for c, v in enumerate(row):
            ref[(*lead, pl.ds(r * SUB, SUB), pl.ds(c * LANES, LANES))] = v


def spread_row(ref, cols, *index):
    *lead, row = index
    return [
        jnp.broadcast_to(ref[(*lead, pl.ds(row, 1), pl.ds(c * LANES, LANES))], (SUB, LANES))
        for c in range(cols)
    ]


def turning(shears, sine, cosine, total_dirs):
    ux, uy, vx, vy = shears
    scale = total_dirs / (2.0 * math.pi)
    return [
        [
            scale
            * (
                sine * cosine * (ux[r][c] - vy[r][c])
                + sine * sine * uy[r][c]
                - cosine * cosine * vx[r][c]
            )
            for c in range(len(ux[0]))
        ]
        for r in range(len(ux))
    ]


def half_sum(a, b):
    return [[0.5 * (x + y) for x, y in zip(p, q)] for p, q in zip(a, b)]


def half_diff(a, b):
    return [[0.5 * (x - y) for x, y in zip(p, q)] for p, q in zip(a, b)]


def shears_of(g, u, v, u_lo, u_hi, v_lo, v_hi):
    ux = half_diff(g.below(u, u_hi), g.above(u, u_lo))
    vx = half_diff(g.below(v, v_hi), g.above(v, v_lo))
    uy = half_diff([g.right(r) for r in u], [g.left(r, 0.0) for r in u])
    vy = half_diff([g.right(r) for r in v], [g.left(r, 0.0) for r in v])
    return ux, uy, vx, vy


COS, SIN, FCOS, FSIN = 0, 6, 12, 17
TABLE = 22


def angle_table(sectors, per):
    total = sectors * per
    step = 2.0 * math.pi / total
    out = np.zeros((sectors, TABLE), np.float64)
    for k in range(sectors):
        d = np.arange(-1, per + 1) + k * per
        out[k, COS : COS + per + 2] = np.cos(d * step)
        out[k, SIN : SIN + per + 2] = np.sin(d * step)
        face = (np.arange(per + 1) + k * per - 0.5) * step
        out[k, FCOS : FCOS + per + 1] = np.cos(face)
        out[k, FSIN : FSIN + per + 1] = np.sin(face)
    return out.astype(np.float32)


HALO = 3


def rows_kernel(x_ref, fld_ref, up_ref, dn_ref):
    last = up_ref.shape[1] - SUB
    sides = ((up_ref, range(16 - HALO, 16)), (dn_ref, range(HALO)))
    for ref, rows in sides:
        for k, row in enumerate(rows):
            ref[k, pl.ds(last, SUB), :] = jnp.zeros((SUB, 2 * LANES), F32)
            for n in range(3):
                ref[k, pl.ds(last + n, 1), :] = fld_ref[n, pl.ds(row, 1), :]

    def one(q, _):
        at = pl.multiple_of(q * SUB, SUB)
        for ref, rows in sides:
            for k, row in enumerate(rows):
                for c in range(2):
                    start = at * 32 + (row // SUB * 2 + c) * SUB + row % SUB
                    v = x_ref[pl.ds(start, SUB, stride=32), :]
                    land = spread_row(fld_ref, 2, 2, row)[c]
                    ref[k, pl.ds(at, SUB), pl.ds(c * LANES, LANES)] = v * land
        return 0

    lax.fori_loop(0, last // SUB, one, 0)


def pack_inner(g, a, b):
    low2 = g.s < 6
    first = jnp.where(low2, roll(a[0], 6, 0), roll(a[1], 6, 0))
    mid = jnp.where(g.s < 4, roll(a[1], 6, 0), roll(b[0], 2, 0))
    last = jnp.where(g.s < 2, roll(b[0], 2, 0), roll(b[1], 2, 0))
    return first, mid, last


def pack_outer(g, a, b):
    one = jnp.where(g.s < 2, a[0], roll(a[1], 4, 0))
    two = jnp.where(g.s < 6, roll(b[0], 4, 0), b[1])
    return jnp.where(g.s < 4, one, two)


def unpack(g, inner, outer):
    a, b, c = inner
    a2, b2, b6, c6, o4 = roll(a, 2, 0), roll(b, 2, 0), roll(b, 6, 0), roll(c, 6, 0), roll(outer, 4, 0)
    low2, low6 = g.s < 2, g.s < 6
    one = [jnp.where(low2, outer, a2), jnp.where(low2, a2, jnp.where(low6, b2, o4))]
    two = [jnp.where(low2, o4, jnp.where(low6, b6, c6)), jnp.where(low6, c6, outer)]
    return one, two


def ends_kernel(total, sec_ref, tab_ref, cg_ref, x_ref, cur_ref, mat_ref,
                prev_ref, next_ref, ub_s, vb_s, vl_s, k_s, *scratch):
    g = Grid()
    sec = sec_ref[0]
    pairs = x_ref.shape[0] // 2
    ends = (0, x_ref.shape[1] - 1)
    zero = [jnp.zeros((SUB, LANES), F32)] * 2
    u, v = tiles(cur_ref, 0), tiles(cur_ref, 1)
    put_tiles(ub_s, half_sum(u, g.below(u, zero)))
    vb = half_sum(v, [g.right(r) for r in v])
    put_tiles(vb_s, vb)
    put_tiles(vl_s, [g.left(vb[r], 0.5 * v[r][0]) for r in range(2)])
    sh = shears_of(g, u, v, zero, zero, zero, zero)
    for n, f in ((0, 0), (1, 4)):
        put_tiles(k_s, turning(sh, tab_ref[sec, FSIN + f], tab_ref[sec, FCOS + f], total), n)

    def speeds(f, d):
        return cg_ref[f] * tab_ref[sec, COS + 1 + d], cg_ref[f] * tab_ref[sec, SIN + 1 + d]

    sub = Substeps(g, ends, speeds, x_ref, cur_ref, mat_ref, ub_s, vb_s, vl_s, scratch)
    edges = lambda pair, n, s: (zero, zero)

    def last(pair, slot):
        for m, (out_ref, limit) in enumerate(((prev_ref, jnp.minimum), (next_ref, jnp.maximum))):
            k = tiles(k_s, m)
            both = []
            for h in range(2):
                t = sub.second(pair, slot, edges, h * 2 + m)
                both.append([[limit(k[r][c], 0.0) * t[r][c] for c in range(2)] for r in range(2)])
            for c in range(2):
                got = pack_inner(g, [both[0][r][c] for r in range(2)], [both[1][r][c] for r in range(2)])
                for q in range(3):
                    out_ref[pair, pl.ds(q * SUB, SUB), pl.ds(c * LANES, LANES)] = got[q]

    sub.load(0, 0)
    sub.first(0, 0, edges)
    sub.load(1, 1)

    def two(q, _):
        for slot in (1, 0):
            pair = q * 2 + 2 - slot
            sub.load(jnp.minimum(pair + 1, pairs - 1), 1 - slot)
            sub.first(pair, slot, edges)
            last(pair - 1, 1 - slot)
        return 0

    lax.fori_loop(0, (pairs - 1) // 2, two, 0)
    last(pairs - 1, 0)


FACE, VROW, VLEFT, LAND, SIDE = 0, 4, 7, 10, 13


def column_rows(g, rows, field, gc, gs):
    m = range(2)
    flux = [
        [face_flux(gc + field(FACE + i)[c], rows[i][c], rows[i + 1][c]) for c in m] for i in range(4)
    ]
    once = []
    for i in range(3):
        dy = col_change(g, rows[i + 1], gs, field(VROW + i), field(VLEFT + i)[0])
        land = field(LAND + i)
        once.append([land[c] * (rows[i + 1][c] - ((flux[i + 1][c] - flux[i][c]) + dy[c])) for c in m])
    again = [
        [face_flux(gc + field(FACE + 1 + i)[c], once[i][c], once[i + 1][c]) for c in m] for i in range(2)
    ]
    dy = col_change(g, once[1], gs, field(VROW + 1), field(VLEFT + 1)[0])
    land = field(LAND + 1)
    twice = [land[c] * (once[1][c] - ((again[1][c] - again[0][c]) + dy[c])) for c in m]
    return flux, again, once, twice


def stress_of(co, k, r, b, n, dirs):
    acc = -0.5 * b if n != 1 else jnp.zeros((SUB, LANES), F32)
    for d in range(dirs):
        q = (
            co[d + 1]
            + jnp.maximum(k[d + 1], 0.0) * (co[d + 2] - co[d + 1])
            + jnp.minimum(k[d], 0.0) * (co[d + 1] - co[d])
        )
        acc = acc + q * r[d]
    return acc


def main_kernel(total, sec_ref, tab_ref, cg_ref, ratio_ref, weight_ref,
                x_ref, cur_ref, mat_ref, top_ref, bot_ref, ownup_ref, owndn_ref,
                part_ref, e0_ref, e3_ref, prev_ref, next_ref, force_ref,
                new_ref, sem, ub_s, vb_s, vl_s, k_s, fld_s, ke_s, st_s, r_s, b_s, re_s, be_s,
                *scratch):
    g = Grid()
    pairs = x_ref.shape[0] // 2
    sec = sec_ref[0]
    freqs = x_ref.shape[0]
    dirs = x_ref.shape[1]

    last = freqs * dirs
    u, v = tiles(cur_ref, 0), tiles(cur_ref, 1)

    def beside_fields(n):
        above = [spread_row(top_ref, 2, q, last + n) for q in range(HALO)]
        below = [spread_row(bot_ref, 2, q, last + n) for q in range(HALO)]
        own = [spread_row(cur_ref, 2, n, q) for q in (0, 1, 14, 15)]
        return above + own[:2], own[2:] + below

    us, vs, ls = (beside_fields(n) for n in range(3))
    put_tiles(ub_s, half_sum(u, g.below(u, us[1][2])))
    vb = half_sum(v, [g.right(r) for r in v])
    put_tiles(vb_s, vb)
    put_tiles(vl_s, [g.left(vb[r], 0.5 * v[r][0]) for r in range(2)])
    for side in range(2):
        for q in range(4):
            put_tiles(fld_s, half_sum([us[side][q]], [us[side][q + 1]]), side, FACE + q)
        for q in range(3):
            vv = vs[side][q + 1]
            put_tiles(fld_s, half_sum([vv], [g.right(vv)]), side, VROW + q)
            put_tiles(fld_s, [[0.5 * w for w in vv]], side, VLEFT + q)
            put_tiles(fld_s, [ls[side][q + 1]], side, LAND + q)
        edge = (
            half_diff([us[side][3]], [us[side][1]]),
            half_diff([g.right(us[side][2])], [g.left(us[side][2], 0.0)]),
            half_diff([vs[side][3]], [vs[side][1]]),
            half_diff([g.right(vs[side][2])], [g.left(vs[side][2], 0.0)]),
        )
        for f in range(dirs + 1):
            k = turning(edge, tab_ref[sec, FSIN + f], tab_ref[sec, FCOS + f], total)
            put_tiles(ke_s, k, side, f)
    sh = shears_of(g, u, v, us[0][2], us[1][2], vs[0][2], vs[1][2])
    for f in range(dirs + 1):
        put_tiles(k_s, turning(sh, tab_ref[sec, FSIN + f], tab_ref[sec, FCOS + f], total), f)
    for ref in (r_s, b_s, re_s, be_s):
        ref[...] = jnp.zeros_like(ref)

    def by_direction(n):
        out = jnp.zeros((SUB, LANES), F32)
        for d in range(dirs):
            out = jnp.where(g.s % dirs == d, tab_ref[sec, n + 1 + d], out)
        return out

    cos_rows, sin_rows = by_direction(COS), by_direction(SIN)

    def beside_rows(pair_at):
        q = jnp.minimum(pair_at, pairs - 1)
        live = jnp.where(pair_at < pairs, 1.0, 0.0)
        at = pl.ds(pl.multiple_of(q * SUB, SUB), SUB)
        pair = lambda a, b: jnp.where(g.s < dirs, a, b)
        f = q * 2
        cg = pair(cg_ref[f], cg_ref[f + 1])
        gc, gs = cg * cos_rows, cg * sin_rows
        w = pair(weight_ref[f] * live, weight_ref[f + 1] * live)
        wr = w * pair(ratio_ref[f], ratio_ref[f + 1])
        row = lambda ref, n: [ref[n, at, pl.ds(c * LANES, LANES)] for c in range(2)]
        above = [row(top_ref, n) for n in range(HALO)]
        below = [row(bot_ref, n) for n in range(HALO)]
        for side, rows in (
            (0, above + [row(owndn_ref, 0), row(owndn_ref, 1)]),
            (1, [row(ownup_ref, 1), row(ownup_ref, 2)] + below),
        ):
            field = lambda n: [fld_s[side, n, :, pl.ds(c * LANES, LANES)] for c in range(2)]
            flux, again, once, twice = column_rows(g, rows, field, gc, gs)
            for c in range(2):
                cc = pl.ds(c * LANES, LANES)
                if side == 0:
                    st_s[0, at, cc] = flux[2][c]
                    st_s[1, at, cc] = again[1][c]
                else:
                    st_s[2, at, cc] = once[1][c]
                re_s[side, :, cc] += wr * twice[c]
                be_s[side, :, cc] += w * twice[c]

    def speeds(f, d):
        return cg_ref[f] * tab_ref[sec, COS + 1 + d], cg_ref[f] * tab_ref[sec, SIN + 1 + d]

    sub = Substeps(
        g, tuple(range(dirs)), speeds, x_ref, cur_ref, mat_ref, ub_s, vb_s, vl_s, scratch
    )

    def edges(pair, n, s):
        group = pl.ds(pl.multiple_of(pair * SUB, SUB), SUB)

        def beside(ref, m):
            return [
                jnp.broadcast_to(ref[m, group, pl.ds(c * LANES, LANES)][n : n + 1], (SUB, LANES))
                for c in range(2)
            ]

        return beside(st_s, s), beside(bot_ref, 0) if s == 0 else beside(st_s, 2)

    def finish(pair, slot):
        outs = [[], []]
        for h in range(2):
            f = pair * 2 + h
            w = weight_ref[f]
            wr = w * ratio_ref[f]
            a2 = [sub.second(pair, slot, edges, h * dirs + d) for d in range(dirs)]
            for r in range(2):
                for c in range(2):
                    here = (pl.ds(r * SUB, SUB), pl.ds(c * LANES, LANES))
                    v = [a2[d][r][c] for d in range(dirs)]
                    for d in range(dirs):
                        r_s[(d, *here)] += wr * v[d]
                    b_s[here] += w * ((v[0] + v[1]) + (v[2] + v[3]))
                    k = [k_s[(n, *here)] for n in range(dirs + 1)]
                    inside = [face_flux(k[d + 1], v[d], v[d + 1]) for d in range(dirs - 1)]
                    new_ref[(f, 0, *here)] = v[1] - (inside[1] - inside[0])
                    new_ref[(f, 1, *here)] = v[2] - (inside[2] - inside[1])
                    e0_ref[(f, *here)] = v[0] - (inside[0] - jnp.minimum(k[0], 0.0) * v[0])
                    e3_ref[(f, *here)] = v[3] - (jnp.maximum(k[4], 0.0) * v[3] - inside[2])
            k0, k4 = tiles(k_s, 0), tiles(k_s, dirs)
            outs[0].append([[jnp.minimum(k0[r][c], 0.0) * a2[0][r][c] for c in range(2)] for r in range(2)])
            outs[1].append([[jnp.maximum(k4[r][c], 0.0) * a2[3][r][c] for c in range(2)] for r in range(2)])
        for ref, ends in ((prev_ref, outs[0]), (next_ref, outs[1])):
            for c in range(2):
                ref[pair, :, pl.ds(c * LANES, LANES)] = pack_outer(
                    g, [ends[0][r][c] for r in range(2)], [ends[1][r][c] for r in range(2)]
                )

    spans = [(0, 16), (16, 16), (32, 16), (48, 2)]

    def put(q):
        span = pl.ds(*spans[q])
        return pltpu.make_async_copy(
            new_ref.at[span], part_ref.at[span, pl.ds(1, dirs - 2)], sem.at[q]
        )

    def two(q, _):
        for slot in (1, 0):
            pair = q * 2 + 2 - slot
            sub.load(jnp.minimum(pair + 1, pairs - 1), 1 - slot)
            sub.first(pair, slot, edges)
            finish(pair - 1, 1 - slot)
            beside_rows(pair + 1)
        return 0

    beside_rows(0)
    beside_rows(1)
    sub.load(0, 0)
    sub.first(0, 0, edges)
    sub.load(1, 1)
    for q in range(3):
        lax.fori_loop(q * 4, q * 4 + 4, two, 0)
        put(q).start()
    finish(pairs - 1, 0)
    put(3).start()

    cs = [tab_ref[sec, COS + n] for n in range(dirs + 2)]
    sn = [tab_ref[sec, SIN + n] for n in range(dirs + 2)]
    coef = (
        [1.0 + a * a for a in cs],
        [a * b for a, b in zip(sn, cs)],
        [1.0 + b * b for b in sn],
    )
    stress, edges = [], []
    for n, co in enumerate(coef):
        now = []
        for r in range(2):
            now.append([])
            for c in range(2):
                here = (pl.ds(r * SUB, SUB), pl.ds(c * LANES, LANES))
                k = [k_s[(m, *here)] for m in range(dirs + 1)]
                now[r].append(
                    stress_of(co, k, [r_s[(d, *here)] for d in range(dirs)], b_s[here], n, dirs)
                )
        stress.append(now)
        both = []
        for side in range(2):
            both.append([])
            for c in range(2):
                cc = pl.ds(c * LANES, LANES)
                rr, bb = re_s[side, :, cc], be_s[side, :, cc]
                spread = lambda v: jnp.broadcast_to(v, (SUB, LANES))
                k = [ke_s[side, m, :, cc] for m in range(dirs + 1)]
                rd = [spread(rr[d : d + 1] + rr[d + dirs : d + dirs + 1]) for d in range(dirs)]
                both[side].append(
                    stress_of(co, k, rd, spread(jnp.sum(bb, axis=0, keepdims=True)), n, dirs)
                )
        edges.append(both)
    xx, xy, yy = stress
    dx = lambda t, e: half_diff(g.below(t, e[1]), g.above(t, e[0]))
    dy = lambda t: half_diff([g.right(r) for r in t], [g.left(r, 0.0) for r in t])
    for n, (p, q) in enumerate(((dx(xx, edges[0]), dy(xy)), (dx(xy, edges[1]), dy(yy)))):
        put_tiles(force_ref, [[-(p[r][c] + q[r][c]) for c in range(2)] for r in range(2)], n)

    for q in range(4):
        put(q).wait()


def join_kernel(e0_ref, e3_ref, inp_ref, inn_ref, outp_ref, outn_ref, part_ref, o_ref, buf, sem):
    g = Grid()
    pairs = inp_ref.shape[0]
    dirs = o_ref.shape[1]
    parts = 5
    step = pairs // parts

    def put(q, n, d):
        span = pl.ds(q * step * 2, step * 2)
        return pltpu.make_async_copy(buf.at[n, span], o_ref.at[span, d], sem.at[q, n])

    for q in range(parts):
        for n, (e_ref, inner_ref, outer_ref, sign, d) in enumerate(
            ((e0_ref, inp_ref, outp_ref, 1.0, 0), (e3_ref, inn_ref, outn_ref, -1.0, dirs - 1))
        ):
            def one(pair, _):
                for c in range(2):
                    cc = pl.ds(c * LANES, LANES)
                    inner = [inner_ref[pair, pl.ds(k * SUB, SUB), cc] for k in range(3)]
                    both = unpack(g, inner, outer_ref[pair, :, cc])
                    for h in range(2):
                        for r in range(2):
                            at = (pair * 2 + h, pl.ds(r * SUB, SUB), cc)
                            buf[(n, *at)] = e_ref[at] + sign * both[h][r]
                return 0

            lax.fori_loop(q * step, (q + 1) * step, one, 0)
            put(q, n, d).start()
    for q in range(parts):
        put(q, 0, 0).wait()
        put(q, 1, dirs - 1).wait()


def per_device(sectors, points, action, currents, land_mask, group_speed, group_ratio, bin_weight):
    freqs, dirs, rows, cols = action.shape
    total = dirs * sectors
    table = jnp.asarray(angle_table(sectors, dirs))
    sec = lax.axis_index("dir").reshape(1).astype(jnp.int32)
    smem = pl.BlockSpec(memory_space=pltpu.SMEM)
    combos = freqs * dirs
    f32 = lambda *s: jax.ShapeDtypeStruct(s, F32)

    def send(value, axis, pairs):
        return lax.ppermute(value, axis, pairs)

    vmem = lambda *s: pltpu.VMEM(s, F32)
    params = lambda: pltpu.CompilerParams(vmem_limit_bytes=24 * 2**20)

    matrix = shift_matrix(cols)
    fields = jnp.concatenate([currents, land_mask.astype(F32)[None]])
    flat = action.reshape(combos, rows // SUB, SUB, cols // LANES, LANES)
    flat = flat.transpose(0, 1, 3, 2, 4).reshape(combos * rows * cols // LANES, LANES)
    vm = pl.BlockSpec(memory_space=pltpu.VMEM)
    hbm = pl.BlockSpec(memory_space=pl.ANY)
    up_rows, dn_rows = pl.pallas_call(
        rows_kernel,
        in_specs=[vm, vm],
        out_specs=[vm, vm],
        out_shape=[f32(HALO, combos + SUB, cols)] * 2,
        compiler_params=params(),
        name="boundary_rows",
    )(flat, fields)
    up = [(i, i + 1) for i in range(points - 1)]
    down = [(j, i) for i, j in up]
    top = send(up_rows, "pts", up)
    bot = send(dn_rows, "pts", down)

    in_prev, in_next = pl.pallas_call(
        functools.partial(ends_kernel, total),
        in_specs=[smem, smem, smem, vm, vm, vm],
        out_specs=[vm, vm],
        out_shape=[f32(freqs // 2, 24, cols)] * 2,
        scratch_shapes=[vmem(rows, cols)] * 3 + [vmem(2, rows, cols)] + substep_scratch(4, cols),
        compiler_params=params(),
        name="sector_ends",
    )(sec, table, group_speed, action, fields, matrix)
    fwd = [(i, (i + 1) % sectors) for i in range(sectors)]
    back = [(j, i) for i, j in fwd]
    inner_from_prev = send(in_next, "dir", fwd)
    inner_from_next = send(in_prev, "dir", back)

    part, e0, e3, out_prev, out_next, force = pl.pallas_call(
        functools.partial(main_kernel, total),
        in_specs=[smem] * 5 + [vm] * 7,
        out_specs=[hbm, vm, vm, vm, vm, vm],
        out_shape=[
            f32(freqs, dirs, rows, cols),
            f32(freqs, rows, cols),
            f32(freqs, rows, cols),
            f32(freqs // 2, SUB, cols),
            f32(freqs // 2, SUB, cols),
            f32(2, rows, cols),
        ],
        scratch_shapes=[
            vmem(freqs, dirs - 2, rows, cols), pltpu.SemaphoreType.DMA((4,)),
            vmem(rows, cols), vmem(rows, cols), vmem(rows, cols), vmem(dirs + 1, rows, cols),
            vmem(2, SIDE, SUB, cols), vmem(2, dirs + 1, SUB, cols), vmem(3, combos, cols),
            vmem(dirs, rows, cols), vmem(rows, cols), vmem(2, SUB, cols), vmem(2, SUB, cols),
            *substep_scratch(2 * dirs, cols),
        ],
        compiler_params=params(),
        name="transport",
    )(sec, table, group_speed, group_ratio, bin_weight, action, fields, matrix,
      top, bot, up_rows, dn_rows)

    outer_from_prev = send(out_next, "dir", fwd)
    outer_from_next = send(out_prev, "dir", back)
    half = sectors // 2
    force = force + send(force, "dir", [(i, (i + half) % sectors) for i in range(sectors)])
    near = [
        send(force, "dir",
             [(i, i // half * half + (i % half + s) % half) for i in range(sectors)])
        for s in range(1, half)
    ]
    force = (force + near[1]) + (near[0] + near[2])

    new_action = pl.pallas_call(
        join_kernel,
        in_specs=[vm] * 6 + [hbm],
        out_specs=hbm,
        out_shape=f32(freqs, dirs, rows, cols),
        input_output_aliases={6: 0},
        scratch_shapes=[vmem(2, freqs, rows, cols), pltpu.SemaphoreType.DMA((5, 2))],
        compiler_params=params(),
        name="join_sectors",
    )(e0, e3, inner_from_prev, inner_from_next, outer_from_prev, outer_from_next, part)
    return new_action, force


def solution(mesh):
    in_specs = (P(None, "dir", "pts", None), P(None, "pts", None), P("pts", None), P(), P(), P())
    out_specs = (P(None, "dir", "pts", None), P(None, "pts", None))

    def body(*args):
        return per_device(mesh.shape["dir"], mesh.shape["pts"], *args)

    return jax.shard_map(body, mesh=mesh, in_specs=in_specs, out_specs=out_specs, check_vma=False)
```

```python
import math
import functools

import numpy as np
import jax
import jax.numpy as jnp
from jax import lax
from jax.sharding import PartitionSpec as P
from jax.experimental import pallas as pl
from jax.experimental.pallas import tpu as pltpu


F32 = jnp.float32
LANES = 128
SUB = 8


def iota_masks():
    s = lax.broadcasted_iota(jnp.int32, (SUB, LANES), 0)
    l = lax.broadcasted_iota(jnp.int32, (SUB, LANES), 1)
    return s, l


def roll(x, shift, axis):
    return pltpu.roll(x, shift, axis)


class Grid:
    def __init__(self):
        s, l = iota_masks()
        self.s = s
        self.first_row = s == 0
        self.last_row = s == SUB - 1
        self.first_col = l == 0
        self.last_col = l == LANES - 1

    def below(self, t, hi):
        n, m = len(t), len(t[0])
        moved = [[roll(t[r][c], SUB - 1, 0) for c in range(m)] for r in range(n)]
        return [
            [
                jnp.where(self.last_row, moved[r + 1][c] if r + 1 < n else hi[c], moved[r][c])
                for c in range(m)
            ]
            for r in range(n)
        ]

    def above(self, t, lo):
        n, m = len(t), len(t[0])
        moved = [[roll(t[r][c], 1, 0) for c in range(m)] for r in range(n)]
        return [
            [
                jnp.where(self.first_row, moved[r - 1][c] if r > 0 else lo[c], moved[r][c])
                for c in range(m)
            ]
            for r in range(n)
        ]

    def right(self, row):
        m = len(row)
        moved = [roll(v, LANES - 1, 1) for v in row]
        return [
            jnp.where(self.last_col, moved[c + 1] if c + 1 < m else 0.0, moved[c]) for c in range(m)
        ]

    def left(self, row, start):
        m = len(row)
        moved = [roll(v, 1, 1) for v in row]
        return [
            jnp.where(self.first_col, moved[c - 1] if c > 0 else start, moved[c]) for c in range(m)
        ]


def face_flux(c, behind, in_front):
    return c * jnp.where(c > 0.0, behind, in_front)


def col_change(g, row, gs, vb, vl):
    right = g.right(row)
    flux = [face_flux(gs + vb[c], row[c], right[c]) for c in range(len(row))]
    edge = jnp.minimum(gs + vl, 0.0) * row[0]
    left = g.left(flux, edge)
    return [flux[c] - left[c] for c in range(len(row))]


def advance(g, t, right, left, gc, gs, ub, vb, vl, land, start, hi):
    n, m = len(t), len(t[0])
    ahead = g.below(t, hi)
    flux = [[face_flux(gc + ub[r][c], t[r][c], ahead[r][c]) for c in range(m)] for r in range(n)]
    before = g.above(flux, start)
    out = []
    for r in range(n):
        out.append([])
        for c in range(m):
            dy = face_flux(gs + vb[r][c], t[r][c], right[r][c]) - face_flux(
                gs + vl[r][c], left[r][c], t[r][c]
            )
            out[r].append(land[r][c] * (t[r][c] - ((flux[r][c] - before[r][c]) + dy)))
    return out


def put_shift_matrix(ref):
    cols = ref.shape[0] // 2
    for c in range(2 * cols // LANES):
        for r in range(cols // LANES):
            at = lax.broadcasted_iota(jnp.int32, (LANES, LANES), 0) + r * LANES
            to = lax.broadcasted_iota(jnp.int32, (LANES, LANES), 1) + c * LANES
            step = 1 if c * LANES < cols else -1
            base = 0 if c * LANES < cols else cols
            v = jnp.where(at - (to - base) == step, 1.0, 0.0).astype(jnp.bfloat16)
            for half in range(2):
                ref[pl.ds(half * cols + r * LANES, LANES), pl.ds(c * LANES, LANES)] = v


def put_halves(ref, t, slot, n):
    cols = len(t[0]) * LANES
    at = pl.ds(n * 2 * SUB, 2 * SUB)
    for c in range(len(t[0])):
        v = jnp.concatenate([t[0][c], t[1][c]], axis=0)
        high = v.astype(jnp.bfloat16)
        low = (v - high.astype(F32)).astype(jnp.bfloat16)
        ref[slot, at, pl.ds(c * LANES, LANES)] = high
        ref[slot, at, pl.ds(cols + c * LANES, LANES)] = low


def block_of(ref, slot, n, first=0):
    return [
        [
            ref[slot, pl.ds((n * 2 + r) * SUB, SUB), pl.ds((first + c) * LANES, LANES)]
            for c in range(2)
        ]
        for r in range(2)
    ]


def put_block(ref, t, slot, n):
    for r in range(2):
        for c in range(2):
            ref[slot, pl.ds((n * 2 + r) * SUB, SUB), pl.ds(c * LANES, LANES)] = t[r][c]


class Substeps:
    def __init__(self, g, dirs, speeds, x_ref, cur_ref, mat_ref, ub_s, vb_s, vl_s, scratch):
        self.g, self.dirs, self.speeds = g, dirs, speeds
        self.x_ref, self.cur_ref, self.mat_ref = x_ref, cur_ref, mat_ref
        self.ub_s, self.vb_s, self.vl_s = ub_s, vb_s, vl_s
        self.t0, self.t1, self.h0, self.h1, self.y0, self.y1 = scratch
        self.members = [(h, d) for h in range(2) for d in dirs]

    def load(self, pair, slot):
        land = tiles(self.cur_ref, 2)
        for n, (h, d) in enumerate(self.members):
            x = tiles(self.x_ref, pair * 2 + h, d)
            t = [[land[r][c] * x[r][c] for c in range(2)] for r in range(2)]
            put_block(self.t0, t, slot, n)
            put_halves(self.h0, t, slot, n)
        self.y0[slot] = jnp.dot(self.h0[slot], self.mat_ref[...], preferred_element_type=F32)

    def step(self, pair, slot, n, t_ref, y_ref, start, hi):
        h, d = self.members[n]
        gc, gs = self.speeds(pair * 2 + h, d)
        return advance(
            self.g, block_of(t_ref, slot, n), block_of(y_ref, slot, n), block_of(y_ref, slot, n, 2),
            gc, gs, tiles(self.ub_s), tiles(self.vb_s), tiles(self.vl_s), tiles(self.cur_ref, 2),
            start, hi,
        )

    def first(self, pair, slot, edges):
        for n in range(len(self.members)):
            t = self.step(pair, slot, n, self.t0, self.y0, *edges(pair, n, 0))
            put_block(self.t1, t, slot, n)
            put_halves(self.h1, t, slot, n)
        self.y1[slot] = jnp.dot(self.h1[slot], self.mat_ref[...], preferred_element_type=F32)

    def second(self, pair, slot, edges, n):
        return self.step(pair, slot, n, self.t1, self.y1, *edges(pair, n, 1))


def substep_scratch(members, cols, slots):
    rows = members * 2 * SUB
    return [
        pltpu.VMEM((slots, rows, cols), F32),
        pltpu.VMEM((slots, rows, cols), F32),
        pltpu.VMEM((slots, rows, 2 * cols), jnp.bfloat16),
        pltpu.VMEM((slots, rows, 2 * cols), jnp.bfloat16),
        pltpu.VMEM((slots, rows, 2 * cols), F32),
        pltpu.VMEM((slots, rows, 2 * cols), F32),
    ]


def tiles(ref, *lead):
    rows, cols = ref.shape[-2] // SUB, ref.shape[-1] // LANES
    return [
        [ref[(*lead, pl.ds(r * SUB, SUB), pl.ds(c * LANES, LANES))] for c in range(cols)]
        for r in range(rows)
    ]


def put_tiles(ref, t, *lead):
    for r, row in enumerate(t):
        for c, v in enumerate(row):
            ref[(*lead, pl.ds(r * SUB, SUB), pl.ds(c * LANES, LANES))] = v


def spread_row(ref, cols, *index):
    *lead, row = index
    return [
        jnp.broadcast_to(ref[(*lead, pl.ds(row, 1), pl.ds(c * LANES, LANES))], (SUB, LANES))
        for c in range(cols)
    ]


def turning(shears, sine, cosine, total_dirs):
    ux, uy, vx, vy = shears
    scale = total_dirs / (2.0 * math.pi)
    return [
        [
            scale
            * (
                sine * cosine * (ux[r][c] - vy[r][c])
                + sine * sine * uy[r][c]
                - cosine * cosine * vx[r][c]
            )
            for c in range(len(ux[0]))
        ]
        for r in range(len(ux))
    ]


def half_sum(a, b):
    return [[0.5 * (x + y) for x, y in zip(p, q)] for p, q in zip(a, b)]


def half_diff(a, b):
    return [[0.5 * (x - y) for x, y in zip(p, q)] for p, q in zip(a, b)]


def shears_of(g, u, v, u_lo, u_hi, v_lo, v_hi):
    ux = half_diff(g.below(u, u_hi), g.above(u, u_lo))
    vx = half_diff(g.below(v, v_hi), g.above(v, v_lo))
    uy = half_diff([g.right(r) for r in u], [g.left(r, 0.0) for r in u])
    vy = half_diff([g.right(r) for r in v], [g.left(r, 0.0) for r in v])
    return ux, uy, vx, vy


COS, SIN, FCOS, FSIN = 0, 6, 12, 17
TABLE = 22


def angle_table(sectors, per):
    total = sectors * per
    step = 2.0 * math.pi / total
    out = np.zeros((sectors, TABLE), np.float64)
    for k in range(sectors):
        d = np.arange(-1, per + 1) + k * per
        out[k, COS : COS + per + 2] = np.cos(d * step)
        out[k, SIN : SIN + per + 2] = np.sin(d * step)
        face = (np.arange(per + 1) + k * per - 0.5) * step
        out[k, FCOS : FCOS + per + 1] = np.cos(face)
        out[k, FSIN : FSIN + per + 1] = np.sin(face)
    return out.astype(np.float32)


HALO = 3


def rows_kernel(x_ref, cur_ref, land_ref, up_ref, dn_ref, fld_ref, keep_ref, mask_ref, sem):
    last = up_ref.shape[1] - SUB
    parts = sem.shape[0] - 2
    count = last // parts
    sides = ((up_ref, range(16 - HALO, 16)), (dn_ref, range(HALO)))

    def fetch(i):
        span = pl.ds(i * count * 32, count * 32)
        return pltpu.make_async_copy(x_ref.at[span], keep_ref.at[span], sem.at[i])

    fields = pltpu.make_async_copy(cur_ref, fld_ref.at[pl.ds(0, 2)], sem.at[parts])
    mask = pltpu.make_async_copy(land_ref, mask_ref, sem.at[parts + 1])
    fields.start()
    mask.start()
    for i in range(parts):
        fetch(i).start()
    fields.wait()
    mask.wait()
    fld_ref[2] = mask_ref[...].astype(F32)
    for ref, rows in sides:
        for k, row in enumerate(rows):
            ref[k, pl.ds(last, SUB), :] = jnp.zeros((SUB, 2 * LANES), F32)
            for n in range(3):
                ref[k, pl.ds(last + n, 1), :] = fld_ref[n, pl.ds(row, 1), :]

    def one(q, _):
        at = pl.multiple_of(q * SUB, SUB)
        for ref, rows in sides:
            for k, row in enumerate(rows):
                for c in range(2):
                    start = at * 32 + (row // SUB * 2 + c) * SUB + row % SUB
                    v = keep_ref[pl.ds(start, SUB, stride=32), :]
                    land = spread_row(fld_ref, 2, 2, row)[c]
                    ref[k, pl.ds(at, SUB), pl.ds(c * LANES, LANES)] = v * land
        return 0

    for i in range(parts):
        fetch(i).wait()
        lax.fori_loop(i * (count // SUB), (i + 1) * (count // SUB), one, 0)


def pack_inner(g, a, b):
    low2 = g.s < 6
    first = jnp.where(low2, roll(a[0], 6, 0), roll(a[1], 6, 0))
    mid = jnp.where(g.s < 4, roll(a[1], 6, 0), roll(b[0], 2, 0))
    last = jnp.where(g.s < 2, roll(b[0], 2, 0), roll(b[1], 2, 0))
    return first, mid, last


def pack_outer(g, a, b):
    one = jnp.where(g.s < 2, a[0], roll(a[1], 4, 0))
    two = jnp.where(g.s < 6, roll(b[0], 4, 0), b[1])
    return jnp.where(g.s < 4, one, two)


def unpack(g, inner, outer):
    a, b, c = inner
    a2, b2, b6, c6, o4 = roll(a, 2, 0), roll(b, 2, 0), roll(b, 6, 0), roll(c, 6, 0), roll(outer, 4, 0)
    low2, low6 = g.s < 2, g.s < 6
    one = [jnp.where(low2, outer, a2), jnp.where(low2, a2, jnp.where(low6, b2, o4))]
    two = [jnp.where(low2, o4, jnp.where(low6, b6, c6)), jnp.where(low6, c6, outer)]
    return one, two


def ends_kernel(total, sec_ref, tab_ref, cg_ref, x_ref, cur_ref,
                prev_ref, next_ref, mat_ref, ub_s, vb_s, vl_s, k_s, *scratch):
    g = Grid()
    sec = sec_ref[0]
    pairs = x_ref.shape[0] // 2
    ends = (0, x_ref.shape[1] - 1)
    put_shift_matrix(mat_ref)
    zero = [jnp.zeros((SUB, LANES), F32)] * 2
    u, v = tiles(cur_ref, 0), tiles(cur_ref, 1)
    put_tiles(ub_s, half_sum(u, g.below(u, zero)))
    vb = half_sum(v, [g.right(r) for r in v])
    put_tiles(vb_s, vb)
    put_tiles(vl_s, [g.left(vb[r], 0.5 * v[r][0]) for r in range(2)])
    sh = shears_of(g, u, v, zero, zero, zero, zero)
    for n, f in ((0, 0), (1, 4)):
        put_tiles(k_s, turning(sh, tab_ref[sec, FSIN + f], tab_ref[sec, FCOS + f], total), n)

    def speeds(f, d):
        return cg_ref[f] * tab_ref[sec, COS + 1 + d], cg_ref[f] * tab_ref[sec, SIN + 1 + d]

    sub = Substeps(g, ends, speeds, x_ref, cur_ref, mat_ref, ub_s, vb_s, vl_s, scratch)
    edges = lambda pair, n, s: (zero, zero)

    def last(pair, slot):
        for m, (out_ref, limit) in enumerate(((prev_ref, jnp.minimum), (next_ref, jnp.maximum))):
            k = tiles(k_s, m)
            both = []
            for h in range(2):
                t = sub.second(pair, slot, edges, h * 2 + m)
                both.append([[limit(k[r][c], 0.0) * t[r][c] for c in range(2)] for r in range(2)])
            for c in range(2):
                got = pack_inner(g, [both[0][r][c] for r in range(2)], [both[1][r][c] for r in range(2)])
                for q in range(3):
                    out_ref[pair, pl.ds(q * SUB, SUB), pl.ds(c * LANES, LANES)] = got[q]

    def turn(p, at):
        sub.load(p + 2, (at + 2) % 3)
        sub.first(p, at, edges)
        last(p - 2, (at + 1) % 3)

    for p in range(4):
        sub.load(p, p % 3)
        if p >= 2:
            sub.first(p - 2, p - 2, edges)

    def three(q, _):
        for n in range(3):
            turn(q * 3 + 2 + n, (2 + n) % 3)
        return 0

    turns = (pairs - 4) // 3
    lax.fori_loop(0, turns, three, 0)
    for p in range(turns * 3 + 2, pairs + 2):
        if p + 2 < pairs:
            sub.load(p + 2, (p + 2) % 3)
        if p < pairs:
            sub.first(p, p % 3, edges)
        last(p - 2, (p - 2) % 3)


FACE, VROW, VLEFT, LAND, SIDE = 0, 4, 7, 10, 13


def column_rows(g, rows, field, gc, gs):
    m = range(2)
    flux = [
        [face_flux(gc + field(FACE + i)[c], rows[i][c], rows[i + 1][c]) for c in m] for i in range(4)
    ]
    once = []
    for i in range(3):
        dy = col_change(g, rows[i + 1], gs, field(VROW + i), field(VLEFT + i)[0])
        land = field(LAND + i)
        once.append([land[c] * (rows[i + 1][c] - ((flux[i + 1][c] - flux[i][c]) + dy[c])) for c in m])
    again = [
        [face_flux(gc + field(FACE + 1 + i)[c], once[i][c], once[i + 1][c]) for c in m] for i in range(2)
    ]
    dy = col_change(g, once[1], gs, field(VROW + 1), field(VLEFT + 1)[0])
    land = field(LAND + 1)
    twice = [land[c] * (once[1][c] - ((again[1][c] - again[0][c]) + dy[c])) for c in m]
    return flux, again, once, twice


def stress_of(co, k, r, b, n, dirs):
    acc = -0.5 * b if n != 1 else jnp.zeros((SUB, LANES), F32)
    for d in range(dirs):
        q = (
            co[d + 1]
            + jnp.maximum(k[d + 1], 0.0) * (co[d + 2] - co[d + 1])
            + jnp.minimum(k[d], 0.0) * (co[d + 1] - co[d])
        )
        acc = acc + q * r[d]
    return acc


def main_kernel(total, sec_ref, tab_ref, cg_ref, ratio_ref, weight_ref,
                x_ref, cur_ref, mat_ref, top_ref, bot_ref, ownup_ref, owndn_ref,
                part_ref, e0_ref, e3_ref, prev_ref, next_ref, force_ref,
                new_ref, sem, ub_s, vb_s, vl_s, k_s, fld_s, ke_s, st_s, r_s, b_s, re_s, be_s,
                *scratch):
    g = Grid()
    pairs = x_ref.shape[0] // 2
    sec = sec_ref[0]
    freqs = x_ref.shape[0]
    dirs = x_ref.shape[1]

    last = freqs * dirs
    u, v = tiles(cur_ref, 0), tiles(cur_ref, 1)

    def beside_fields(n):
        above = [spread_row(top_ref, 2, q, last + n) for q in range(HALO)]
        below = [spread_row(bot_ref, 2, q, last + n) for q in range(HALO)]
        own = [spread_row(cur_ref, 2, n, q) for q in (0, 1, 14, 15)]
        return above + own[:2], own[2:] + below

    us, vs, ls = (beside_fields(n) for n in range(3))
    put_tiles(ub_s, half_sum(u, g.below(u, us[1][2])))
    vb = half_sum(v, [g.right(r) for r in v])
    put_tiles(vb_s, vb)
    put_tiles(vl_s, [g.left(vb[r], 0.5 * v[r][0]) for r in range(2)])
    for side in range(2):
        for q in range(4):
            put_tiles(fld_s, half_sum([us[side][q]], [us[side][q + 1]]), side, FACE + q)
        for q in range(3):
            vv = vs[side][q + 1]
            put_tiles(fld_s, half_sum([vv], [g.right(vv)]), side, VROW + q)
            put_tiles(fld_s, [[0.5 * w for w in vv]], side, VLEFT + q)
            put_tiles(fld_s, [ls[side][q + 1]], side, LAND + q)
        edge = (
            half_diff([us[side][3]], [us[side][1]]),
            half_diff([g.right(us[side][2])], [g.left(us[side][2], 0.0)]),
            half_diff([vs[side][3]], [vs[side][1]]),
            half_diff([g.right(vs[side][2])], [g.left(vs[side][2], 0.0)]),
        )
        for f in range(dirs + 1):
            k = turning(edge, tab_ref[sec, FSIN + f], tab_ref[sec, FCOS + f], total)
            put_tiles(ke_s, k, side, f)
    sh = shears_of(g, u, v, us[0][2], us[1][2], vs[0][2], vs[1][2])
    for f in range(dirs + 1):
        put_tiles(k_s, turning(sh, tab_ref[sec, FSIN + f], tab_ref[sec, FCOS + f], total), f)
    for ref in (r_s, b_s, re_s, be_s):
        ref[...] = jnp.zeros_like(ref)

    def by_direction(n):
        out = jnp.zeros((SUB, LANES), F32)
        for d in range(dirs):
            out = jnp.where(g.s % dirs == d, tab_ref[sec, n + 1 + d], out)
        return out

    cos_rows, sin_rows = by_direction(COS), by_direction(SIN)

    def beside_rows(pair_at):
        q = jnp.minimum(pair_at, pairs - 1)
        live = jnp.where(pair_at < pairs, 1.0, 0.0)
        at = pl.ds(pl.multiple_of(q * SUB, SUB), SUB)
        pair = lambda a, b: jnp.where(g.s < dirs, a, b)
        f = q * 2
        cg = pair(cg_ref[f], cg_ref[f + 1])
        gc, gs = cg * cos_rows, cg * sin_rows
        w = pair(weight_ref[f] * live, weight_ref[f + 1] * live)
        wr = w * pair(ratio_ref[f], ratio_ref[f + 1])
        row = lambda ref, n: [ref[n, at, pl.ds(c * LANES, LANES)] for c in range(2)]
        above = [row(top_ref, n) for n in range(HALO)]
        below = [row(bot_ref, n) for n in range(HALO)]
        for side, rows in (
            (0, above + [row(owndn_ref, 0), row(owndn_ref, 1)]),
            (1, [row(ownup_ref, 1), row(ownup_ref, 2)] + below),
        ):
            field = lambda n: [fld_s[side, n, :, pl.ds(c * LANES, LANES)] for c in range(2)]
            flux, again, once, twice = column_rows(g, rows, field, gc, gs)
            for c in range(2):
                cc = pl.ds(c * LANES, LANES)
                if side == 0:
                    st_s[0, at, cc] = flux[2][c]
                    st_s[1, at, cc] = again[1][c]
                else:
                    st_s[2, at, cc] = once[1][c]
                re_s[side, :, cc] += wr * twice[c]
                be_s[side, :, cc] += w * twice[c]

    def speeds(f, d):
        return cg_ref[f] * tab_ref[sec, COS + 1 + d], cg_ref[f] * tab_ref[sec, SIN + 1 + d]

    sub = Substeps(
        g, tuple(range(dirs)), speeds, x_ref, cur_ref, mat_ref, ub_s, vb_s, vl_s, scratch
    )

    def edges(pair, n, s):
        group = pl.ds(pl.multiple_of(pair * SUB, SUB), SUB)

        def beside(ref, m):
            return [
                jnp.broadcast_to(ref[m, group, pl.ds(c * LANES, LANES)][n : n + 1], (SUB, LANES))
                for c in range(2)
            ]

        return beside(st_s, s), beside(bot_ref, 0) if s == 0 else beside(st_s, 2)

    def finish(pair, slot):
        outs = [[], []]
        for h in range(2):
            f = pair * 2 + h
            w = weight_ref[f]
            wr = w * ratio_ref[f]
            a2 = [sub.second(pair, slot, edges, h * dirs + d) for d in range(dirs)]
            for r in range(2):
                for c in range(2):
                    here = (pl.ds(r * SUB, SUB), pl.ds(c * LANES, LANES))
                    v = [a2[d][r][c] for d in range(dirs)]
                    for d in range(dirs):
                        r_s[(d, *here)] += wr * v[d]
                    b_s[here] += w * ((v[0] + v[1]) + (v[2] + v[3]))
                    k = [k_s[(n, *here)] for n in range(dirs + 1)]
                    inside = [face_flux(k[d + 1], v[d], v[d + 1]) for d in range(dirs - 1)]
                    new_ref[(f, 0, *here)] = v[1] - (inside[1] - inside[0])
                    new_ref[(f, 1, *here)] = v[2] - (inside[2] - inside[1])
                    e0_ref[(f, *here)] = v[0] - (inside[0] - jnp.minimum(k[0], 0.0) * v[0])
                    e3_ref[(f, *here)] = v[3] - (jnp.maximum(k[4], 0.0) * v[3] - inside[2])
            k0, k4 = tiles(k_s, 0), tiles(k_s, dirs)
            outs[0].append([[jnp.minimum(k0[r][c], 0.0) * a2[0][r][c] for c in range(2)] for r in range(2)])
            outs[1].append([[jnp.maximum(k4[r][c], 0.0) * a2[3][r][c] for c in range(2)] for r in range(2)])
        for ref, ends in ((prev_ref, outs[0]), (next_ref, outs[1])):
            for c in range(2):
                ref[pair, :, pl.ds(c * LANES, LANES)] = pack_outer(
                    g, [ends[0][r][c] for r in range(2)], [ends[1][r][c] for r in range(2)]
                )

    spans = [(0, 16), (16, 16), (32, 16), (48, 2)]

    def put(q):
        span = pl.ds(*spans[q])
        return pltpu.make_async_copy(
            new_ref.at[span], part_ref.at[span, pl.ds(1, dirs - 2)], sem.at[q]
        )

    def two(q, _):
        for slot in (1, 0):
            pair = q * 2 + 2 - slot
            sub.load(jnp.minimum(pair + 1, pairs - 1), 1 - slot)
            sub.first(pair, slot, edges)
            finish(pair - 1, 1 - slot)
            beside_rows(pair + 1)
        return 0

    beside_rows(0)
    beside_rows(1)
    sub.load(0, 0)
    sub.first(0, 0, edges)
    sub.load(1, 1)
    for q in range(3):
        lax.fori_loop(q * 4, q * 4 + 4, two, 0)
        put(q).start()
    finish(pairs - 1, 0)
    put(3).start()

    cs = [tab_ref[sec, COS + n] for n in range(dirs + 2)]
    sn = [tab_ref[sec, SIN + n] for n in range(dirs + 2)]
    coef = (
        [1.0 + a * a for a in cs],
        [a * b for a, b in zip(sn, cs)],
        [1.0 + b * b for b in sn],
    )
    stress, edges = [], []
    for n, co in enumerate(coef):
        now = []
        for r in range(2):
            now.append([])
            for c in range(2):
                here = (pl.ds(r * SUB, SUB), pl.ds(c * LANES, LANES))
                k = [k_s[(m, *here)] for m in range(dirs + 1)]
                now[r].append(
                    stress_of(co, k, [r_s[(d, *here)] for d in range(dirs)], b_s[here], n, dirs)
                )
        stress.append(now)
        both = []
        for side in range(2):
            both.append([])
            for c in range(2):
                cc = pl.ds(c * LANES, LANES)
                rr, bb = re_s[side, :, cc], be_s[side, :, cc]
                spread = lambda v: jnp.broadcast_to(v, (SUB, LANES))
                k = [ke_s[side, m, :, cc] for m in range(dirs + 1)]
                rd = [spread(rr[d : d + 1] + rr[d + dirs : d + dirs + 1]) for d in range(dirs)]
                both[side].append(
                    stress_of(co, k, rd, spread(jnp.sum(bb, axis=0, keepdims=True)), n, dirs)
                )
        edges.append(both)
    xx, xy, yy = stress
    dx = lambda t, e: half_diff(g.below(t, e[1]), g.above(t, e[0]))
    dy = lambda t: half_diff([g.right(r) for r in t], [g.left(r, 0.0) for r in t])
    for n, (p, q) in enumerate(((dx(xx, edges[0]), dy(xy)), (dx(xy, edges[1]), dy(yy)))):
        put_tiles(force_ref, [[-(p[r][c] + q[r][c]) for c in range(2)] for r in range(2)], n)

    for q in range(4):
        put(q).wait()


def join_kernel(e0_ref, e3_ref, inp_ref, inn_ref, outp_ref, outn_ref, part_ref, o_ref, buf, sem):
    g = Grid()
    pairs = inp_ref.shape[0]
    dirs = o_ref.shape[1]
    parts = 5
    step = pairs // parts

    def put(q, n, d):
        span = pl.ds(q * step * 2, step * 2)
        return pltpu.make_async_copy(buf.at[n, span], o_ref.at[span, d], sem.at[q, n])

    for q in range(parts):
        for n, (e_ref, inner_ref, outer_ref, sign, d) in enumerate(
            ((e0_ref, inp_ref, outp_ref, 1.0, 0), (e3_ref, inn_ref, outn_ref, -1.0, dirs - 1))
        ):
            def one(pair, _):
                for c in range(2):
                    cc = pl.ds(c * LANES, LANES)
                    inner = [inner_ref[pair, pl.ds(k * SUB, SUB), cc] for k in range(3)]
                    both = unpack(g, inner, outer_ref[pair, :, cc])
                    for h in range(2):
                        for r in range(2):
                            at = (pair * 2 + h, pl.ds(r * SUB, SUB), cc)
                            buf[(n, *at)] = e_ref[at] + sign * both[h][r]
                return 0

            lax.fori_loop(q * step, (q + 1) * step, one, 0)
            put(q, n, d).start()
    for q in range(parts):
        put(q, 0, 0).wait()
        put(q, 1, dirs - 1).wait()


def per_device(sectors, points, action, currents, land_mask, group_speed, group_ratio, bin_weight):
    freqs, dirs, rows, cols = action.shape
    total = dirs * sectors
    table = jnp.asarray(angle_table(sectors, dirs))
    sec = lax.axis_index("dir").reshape(1).astype(jnp.int32)
    smem = pl.BlockSpec(memory_space=pltpu.SMEM)
    combos = freqs * dirs
    f32 = lambda *s: jax.ShapeDtypeStruct(s, F32)

    def send(value, axis, pairs):
        return lax.ppermute(value, axis, pairs)

    vmem = lambda *s: pltpu.VMEM(s, F32)
    params = lambda: pltpu.CompilerParams(vmem_limit_bytes=24 * 2**20)
    fast = lambda: pltpu.CompilerParams(vmem_limit_bytes=24 * 2**20)

    flat = action.reshape(combos, rows // SUB, SUB, cols // LANES, LANES)
    flat = flat.transpose(0, 1, 3, 2, 4).reshape(combos * rows * cols // LANES, LANES)
    vm = pl.BlockSpec(memory_space=pltpu.VMEM)
    hbm = pl.BlockSpec(memory_space=pl.ANY)
    up_rows, dn_rows, fields = pl.pallas_call(
        rows_kernel,
        in_specs=[hbm] * 3,
        out_specs=[vm] * 3,
        out_shape=[f32(HALO, combos + SUB, cols)] * 2 + [f32(3, rows, cols)],
        scratch_shapes=[
            vmem(flat.shape[0] + 32, LANES), pltpu.VMEM((rows, cols), jnp.int32), pltpu.SemaphoreType.DMA((7,))
        ],
        compiler_params=pltpu.CompilerParams(vmem_limit_bytes=60 * 2**20),
        name="boundary_rows",
    )(flat, currents, land_mask)
    up = [(i, i + 1) for i in range(points - 1)]
    down = [(j, i) for i, j in up]
    top = send(up_rows, "pts", up)
    bot = send(dn_rows, "pts", down)

    in_prev, in_next, matrix = pl.pallas_call(
        functools.partial(ends_kernel, total),
        in_specs=[smem, smem, smem, vm, vm],
        out_specs=[vm, vm, vm],
        out_shape=[f32(freqs // 2, 24, cols)] * 2
        + [jax.ShapeDtypeStruct((2 * cols, 2 * cols), jnp.bfloat16)],
        scratch_shapes=[vmem(rows, cols)] * 3 + [vmem(2, rows, cols)] + substep_scratch(4, cols, 3),
        compiler_params=fast(),
        name="sector_ends",
    )(sec, table, group_speed, action, fields)
    fwd = [(i, (i + 1) % sectors) for i in range(sectors)]
    back = [(j, i) for i, j in fwd]
    inner_from_prev = send(in_next, "dir", fwd)
    inner_from_next = send(in_prev, "dir", back)

    part, e0, e3, out_prev, out_next, force = pl.pallas_call(
        functools.partial(main_kernel, total),
        in_specs=[smem] * 5 + [vm] * 7,
        out_specs=[hbm, vm, vm, vm, vm, vm],
        out_shape=[
            f32(freqs, dirs, rows, cols),
            f32(freqs, rows, cols),
            f32(freqs, rows, cols),
            f32(freqs // 2, SUB, cols),
            f32(freqs // 2, SUB, cols),
            f32(2, rows, cols),
        ],
        scratch_shapes=[
            vmem(freqs, dirs - 2, rows, cols), pltpu.SemaphoreType.DMA((4,)),
            vmem(rows, cols), vmem(rows, cols), vmem(rows, cols), vmem(dirs + 1, rows, cols),
            vmem(2, SIDE, SUB, cols), vmem(2, dirs + 1, SUB, cols), vmem(3, combos, cols),
            vmem(dirs, rows, cols), vmem(rows, cols), vmem(2, SUB, cols), vmem(2, SUB, cols),
            *substep_scratch(2 * dirs, cols, 2),
        ],
        compiler_params=fast(),
        name="transport",
    )(sec, table, group_speed, group_ratio, bin_weight, action, fields, matrix,
      top, bot, up_rows, dn_rows)

    outer_from_prev = send(out_next, "dir", fwd)
    outer_from_next = send(out_prev, "dir", back)
    half = sectors // 2
    force = force + send(force, "dir", [(i, (i + half) % sectors) for i in range(sectors)])
    near = [
        send(force, "dir",
             [(i, i // half * half + (i % half + s) % half) for i in range(sectors)])
        for s in range(1, half)
    ]
    force = (force + near[1]) + (near[0] + near[2])

    new_action = pl.pallas_call(
        join_kernel,
        in_specs=[vm] * 6 + [hbm],
        out_specs=hbm,
        out_shape=f32(freqs, dirs, rows, cols),
        input_output_aliases={6: 0},
        scratch_shapes=[vmem(2, freqs, rows, cols), pltpu.SemaphoreType.DMA((5, 2))],
        compiler_params=params(),
        name="join_sectors",
    )(e0, e3, inner_from_prev, inner_from_next, outer_from_prev, outer_from_next, part)
    return new_action, force


def solution(mesh):
    in_specs = (P(None, "dir", "pts", None), P(None, "pts", None), P("pts", None), P(), P(), P())
    out_specs = (P(None, "dir", "pts", None), P(None, "pts", None))

    def body(*args):
        return per_device(mesh.shape["dir"], mesh.shape["pts"], *args)

    return jax.shard_map(body, mesh=mesh, in_specs=in_specs, out_specs=out_specs, check_vma=False)
```
